128 devices in a mesh: dp: 4 (over x_hi, core), ctx: 32 (over z, y, x_lo).
Axes of the slice: x: 4 (x_hi: 2, x_lo: 2; x = x_hi * 2 + x_lo), y: 4, z: 4, core: 2. Of those that a mesh axis runs over, the one named last changes fastest.
Arguments:
- gate_input: bfloat16 [4, 4096, 4096], P('dp', 'ctx'), may hold values from -6 to 6
- values: bfloat16 [4, 4096, 4096], P('dp', 'ctx'), may hold values from -6 to 6
- cotangent: bfloat16 [4, 4096, 4096], P('dp', 'ctx'), may hold values from -6 to 6
- filter_taps: float32 [4096, 4096], P(('dp', 'ctx')), may hold values from -4 to 4
Outputs:
- output: bfloat16 [4, 4096, 4096], P('dp', 'ctx')
- gate_grad: bfloat16 [4, 4096, 4096], P('dp', 'ctx')
- values_grad: bfloat16 [4, 4096, 4096], P('dp', 'ctx')
- filter_grad: float32 [4096, 4096], P(('dp', 'ctx'))
The draws below stay inside these ranges and needn't reach their ends.
All inputs are finite; a program needn't handle non-finite values.
Results may differ from the reference program's by a relative error of at most 0.013.
Values may be sent and summed in bfloat16 or wider, within the bound.
No kernel may reach another device: no remote copies, remote signals or barrier semaphores. Data moves between devices by JAX's collectives and lax.ppermute only.
A program may use at most 128 MiB of HBM per device.

```python
import math
import jax
import jax.numpy as jnp
from jax import lax

CHANNELS = 4096
SEQ_LEN = 4096
BATCH = 4


def draw_filter_taps(key, part):
    rate_key, noise_key = jax.random.split(jax.random.fold_in(key, 11))
    positions = jnp.arange(SEQ_LEN, dtype=jnp.float32)[:, None]
    log_decay = jax.random.uniform(rate_key, (1, CHANNELS), jnp.float32, math.log(30.0), math.log(SEQ_LEN * 4.0))
    noise = jnp.clip(jax.random.normal(noise_key, (SEQ_LEN, CHANNELS), jnp.float32), -4.0, 4.0)
    decay_length = jnp.exp(log_decay)
    normalizer = jnp.sqrt((1.0 - jnp.exp(-2.0 / decay_length)) / (1.0 - jnp.exp(-2.0 * SEQ_LEN / decay_length)))
    return noise * jnp.exp(-positions / decay_length) * normalizer


def block_scale(key, extent, cuts, smallest, high):
    level = 1.0
    for axis_at, shards_of in cuts:
        steps = jax.random.uniform(jax.random.fold_in(jax.random.fold_in(key, 6), axis_at), (shards_of,), jnp.float32, smallest / len(cuts), high / len(cuts))
        level = level * jnp.repeat(jnp.exp(steps), extent[axis_at] // shards_of).reshape((-1,) + (1,) * (len(extent) - 1 - axis_at))
    return level


def scatter_about(stream_key, shape, spread, reach, cuts=(), kind=jnp.bfloat16):
    values = jax.random.normal(stream_key, shape, jnp.float32) * spread
    if len(cuts) > 0:
        values = block_scale(stream_key, shape, cuts, -0.22, 0.18) * values
    return jnp.clip(values, min=-reach, max=reach).astype(kind)


def setup_inputs(seed: int = 0) -> dict:
    key_list = jax.random.split(jax.random.key(seed), 5)
    gate_input = scatter_about(key_list[0], (BATCH, SEQ_LEN, CHANNELS), 1.0, 6.0, ((0, 4), (1, 32)))
    values = scatter_about(key_list[1], (BATCH, SEQ_LEN, CHANNELS), 1.0, 6.0, ((0, 4), (1, 32)))
    cotangent = scatter_about(key_list[2], (BATCH, SEQ_LEN, CHANNELS), 1.0, 6.0, ((0, 4), (1, 32)))
    filter_taps = draw_filter_taps(jax.random.fold_in(key_list[4], 71), 0)
    return dict(gate_input=gate_input, values=values, cotangent=cotangent, filter_taps=filter_taps)


def dft_tables(blocks, freq_len):
    half_blocks = blocks // 2
    row_index = jnp.arange(half_blocks, dtype=jnp.int32)[:, None]
    freq_index = jnp.arange(blocks, dtype=jnp.int32)[None, :]
    angles = ((row_index * freq_index) % blocks).astype(jnp.float32) * (2.0 * math.pi / blocks)
    first_forward = jnp.stack([jnp.cos(angles), -jnp.sin(angles)], axis=1).astype(jnp.bfloat16)
    first_inverse = jnp.stack([jnp.cos(angles).T, -jnp.sin(angles).T], axis=0).astype(jnp.bfloat16)
    block_index = jnp.arange(blocks, dtype=jnp.int32)[:, None]
    lane_index = jnp.arange(128, dtype=jnp.int32)[None, :]
    twist_angles = ((block_index * lane_index) % freq_len).astype(jnp.float32) * (2.0 * math.pi / freq_len)
    twist_cosine = jnp.cos(twist_angles)[:, :, None]
    twist_sine = jnp.sin(twist_angles)[:, :, None]
    inner_index = jnp.arange(128, dtype=jnp.int32)
    inner_angles = ((inner_index[:, None] * inner_index[None, :]) % 128).astype(jnp.float32) * (2.0 * math.pi / 128)
    cosine = jnp.cos(inner_angles)
    sine_part = jnp.sin(inner_angles)
    second_forward = jnp.stack([jnp.stack([cosine, -sine_part], axis=1), jnp.stack([sine_part, cosine], axis=1)], axis=0).astype(jnp.bfloat16)
    second_inverse = jnp.stack([jnp.stack([cosine, sine_part], axis=1), jnp.stack([-sine_part, cosine], axis=1)], axis=0).astype(jnp.bfloat16)
    return (first_forward, first_inverse, twist_cosine, twist_sine, second_forward, second_inverse)


def product(einsum_form, left_side, right_side):
    return jnp.einsum(einsum_form, left_side.astype(jnp.float32), right_side.astype(jnp.float32), precision=lax.Precision.HIGHEST)


def spectrum(signal, tables):
    grouped = signal.reshape(-1, 128, signal.shape[-1])
    first = product("abc,arp->rpbc", grouped, tables[0])
    twisted = jnp.stack([first[0] * tables[2] + first[1] * tables[3], first[1] * tables[2] - first[0] * tables[3]]).astype(jnp.bfloat16)
    return product("rpbc,rbsq->spqc", twisted, tables[4])


def inverse(spectrum_half, tables, norm_scale):
    mixture = product("rpqc,rqsb->spbc", spectrum_half, tables[5])
    twisted = jnp.stack([mixture[0] * tables[2] - mixture[1] * tables[3], mixture[1] * tables[2] + mixture[0] * tables[3]]).astype(jnp.bfloat16)
    rows = product("rpbc,rpa->abc", twisted, tables[1]) * norm_scale
    return rows.reshape(-1, rows.shape[-1])


def times_spec(left_spec, right_spec):
    return jnp.stack([left_spec[0] * right_spec[0] - left_spec[1] * right_spec[1], left_spec[0] * right_spec[1] + left_spec[1] * right_spec[0]]).astype(jnp.bfloat16)


def times_conj(left_spec, right_spec):
    return jnp.stack([left_spec[0] * right_spec[0] + left_spec[1] * right_spec[1], left_spec[1] * right_spec[0] - left_spec[0] * right_spec[1]]).astype(jnp.bfloat16)


def reference(gate_input, values, cotangent, filter_taps):
    batch_size = gate_input.shape[0]
    seq_len = gate_input.shape[1]
    channels = gate_input.shape[2]
    freq_len = 2 * seq_len
    blocks = seq_len // 64
    tables = dft_tables(blocks, freq_len)
    norm_scale = 1.0 / freq_len
    conv_grad = (cotangent.astype(jnp.float32) * gate_input.astype(jnp.float32)).astype(jnp.bfloat16)
    group_width = min(128, channels)
    group_count = channels // group_width
    value_groups = values.reshape(batch_size, seq_len, group_count, group_width).transpose(2, 0, 1, 3)
    grad_groups = conv_grad.reshape(batch_size, seq_len, group_count, group_width).transpose(2, 0, 1, 3)
    filter_groups = filter_taps.astype(jnp.bfloat16).reshape(seq_len, group_count, group_width).transpose(1, 0, 2)

    def per_group(inputs):
        value_block, grad_block, filter_block = inputs
        filter_spec = spectrum(filter_block, tables)
        conv_list = []
        back_list = []
        taps_sum = jnp.zeros((seq_len, group_width), jnp.float32)
        for member in range(batch_size):
            value_spec = spectrum(value_block[member], tables)
            conv_list.append(inverse(times_spec(value_spec, filter_spec), tables, norm_scale).astype(jnp.bfloat16))
            grad_spec = spectrum(grad_block[member], tables)
            back_list.append(inverse(times_conj(grad_spec, filter_spec), tables, norm_scale).astype(jnp.bfloat16))
            taps_sum = taps_sum + inverse(times_conj(grad_spec, value_spec), tables, norm_scale)
        return jnp.stack(conv_list), jnp.stack(back_list), taps_sum

    conv_groups, back_groups, taps_groups = lax.map(per_group, (value_groups, grad_groups, filter_groups))
    conv = conv_groups.transpose(1, 2, 0, 3).reshape(batch_size, seq_len, channels)
    values_grad = back_groups.transpose(1, 2, 0, 3).reshape(batch_size, seq_len, channels)
    filter_grad = taps_groups.transpose(1, 0, 2).reshape(seq_len, channels)
    output = (gate_input.astype(jnp.float32) * conv.astype(jnp.float32)).astype(jnp.bfloat16)
    gate_grad = (cotangent.astype(jnp.float32) * conv.astype(jnp.float32)).astype(jnp.bfloat16)
    return (output, gate_grad, values_grad, filter_grad)
```

```python
import functools
import math

import jax
import jax.numpy as jnp
import ml_dtypes
import numpy as np
from jax import lax
from jax.experimental import pallas as pl
from jax.experimental.pallas import tpu as pltpu
from jax.sharding import PartitionSpec as P

LANES = 128
PACK = 16
BF16 = jnp.bfloat16
F32 = jnp.float32


def angle_tables(top, bottom, period):
    angles = (np.outer(top, bottom) % period).astype(np.float64) * (2.0 * math.pi / period)
    return np.cos(angles).astype(np.float32), np.sin(angles).astype(np.float32)


def block_diagonal(table):
    eye = np.eye(PACK, dtype=np.float32)
    return np.kron(table, eye).astype(ml_dtypes.bfloat16)


def dft_tables(blocks):
    freq_len = blocks * LANES
    half = blocks // 2
    cosine, sine = angle_tables(np.arange(blocks), np.arange(half), blocks)
    first = np.zeros((blocks, half), np.float32)
    first[0] = cosine[0]
    first[1] = cosine[half]
    for p in range(1, half):
        first[2 * p] = cosine[p]
        first[2 * p + 1] = -sine[p]
    weight = np.full((blocks,), 2.0 / freq_len, np.float32)
    weight[:2] = 1.0 / freq_len
    last = (first * weight[:, None]).T
    twist_cosine, twist_sine = angle_tables(np.arange(half + 1), np.arange(LANES), freq_len)
    inner_cosine, inner_sine = angle_tables(np.arange(LANES), np.arange(LANES), LANES)
    forward = np.block([[inner_cosine, -inner_sine], [inner_sine, inner_cosine]])
    inverse = np.block([[inner_cosine, inner_sine], [-inner_sine, inner_cosine]])
    return (
        block_diagonal(first),
        block_diagonal(last),
        twist_cosine[:, None, :],
        twist_sine[:, None, :],
        forward.astype(ml_dtypes.bfloat16),
        inverse.astype(ml_dtypes.bfloat16),
    )


def swap_lane_groups(pieces):
    count = len(pieces)
    width = LANES // count
    group = lax.broadcasted_iota(jnp.int32, pieces[0].shape, pieces[0].ndim - 1) // width
    results = []
    for g in range(count):
        total = None
        for k in range(count):
            shift = (width * (k - g)) % LANES
            moved = pieces[k] if shift == 0 else pltpu.roll(pieces[k], shift, pieces[k].ndim - 1)
            total = moved if total is None else jnp.where(group == k, moved, total)
        results.append(total)
    return results


def pack_kernel(gate_ref, values_ref, cotangent_ref, taps_ref, packed_ref):
    columns = values_ref.shape[-1]
    per_peer = 32
    peers = columns // per_peer
    flipped = values_ref[0].T
    packed_ref[:, 0:per_peer, :] = flipped.reshape(peers, per_peer, LANES)
    grad = (cotangent_ref[0].astype(F32) * gate_ref[0].astype(F32)).astype(BF16)
    packed_ref[:, per_peer : 2 * per_peer, :] = grad.T.reshape(peers, per_peer, LANES)
    taps = taps_ref[...]
    stacked = jnp.concatenate([taps[:, LANES * n : LANES * (n + 1)] for n in range(4)], axis=0)
    turned = stacked.T.reshape(4, 4, 8, LANES)
    pieces = swap_lane_groups([turned[:, k] for k in range(4)])
    for n in range(4):
        packed_ref[4 * n : 4 * n + 4, 2 * per_peer : 2 * per_peer + 8, :] = pieces[n].astype(BF16)


def unpack_kernel(gate_ref, cotangent_ref, packed_ref, output_ref, gate_grad_ref, values_grad_ref, taps_ref):
    columns = output_ref.shape[-1]
    per_peer = 32
    conv = packed_ref[:, 0:per_peer, :].reshape(columns, LANES).T.astype(F32)
    output_ref[0] = (gate_ref[0].astype(F32) * conv).astype(BF16)
    gate_grad_ref[0] = (cotangent_ref[0].astype(F32) * conv).astype(BF16)
    values_grad_ref[0] = packed_ref[:, per_peer : 2 * per_peer, :].reshape(columns, LANES).T
    taps = packed_ref[:, 2 * per_peer : 2 * per_peer + 8, :].astype(F32)
    pieces = swap_lane_groups([taps[4 * n : 4 * n + 4] for n in range(4)])
    stacked = jnp.stack(pieces, axis=1).reshape(LANES, LANES).T
    for n in range(4):
        taps_ref[:, LANES * n : LANES * (n + 1)] = stacked[32 * n : 32 * n + 32, :]


def conv_kernel(
    data_ref, first_ref, last_ref, cosine_ref, sine_ref, forward_ref, inverse_ref, out_ref,
    filter_ref, twisted_ref, mixed_ref,
):
    half = 32
    rows = twisted_ref.shape[1]

    taps = data_ref[:, 64:72, :].astype(F32).reshape(half, 4, 8, LANES)
    pieces = swap_lane_groups([taps[:, m] for m in range(4)])
    for k in range(4):
        filter_ref[:, 8 * k : 8 * k + 8, :] = pieces[k]

    def first_section(left, right, row):
        both = jnp.concatenate([left.reshape(half * PACK, LANES), right.reshape(half * PACK, LANES)], axis=1)
        rows_out = jnp.dot(first_ref[...], both, preferred_element_type=F32)
        for p in range(half + 1):
            for side in range(2):
                lanes = slice(LANES * side, LANES * (side + 1))
                target = pl.ds(row + PACK * side, PACK)
                if p == 0:
                    real = rows_out[0:PACK, lanes]
                    imag = jnp.zeros((PACK, LANES), F32)
                elif p == half:
                    part = rows_out[PACK : 2 * PACK, lanes]
                    real = part * cosine_ref[p]
                    imag = -part * sine_ref[p]
                else:
                    start = 2 * p * PACK
                    first = rows_out[start : start + PACK, lanes]
                    second = rows_out[start + PACK : start + 2 * PACK, lanes]
                    real = first * cosine_ref[p] + second * sine_ref[p]
                    imag = second * cosine_ref[p] - first * sine_ref[p]
                twisted_ref[p, target, 0:LANES] = real.astype(BF16)
                twisted_ref[p, target, LANES : 2 * LANES] = imag.astype(BF16)

    def signal_step(t, carry):
        kind = t // 4
        member = t % 4
        places = pl.ds(pl.multiple_of(member * half, half), half)
        column = pl.multiple_of(kind * half, half)
        left = data_ref[places, pl.ds(column, PACK), :]
        right = data_ref[places, pl.ds(column + PACK, PACK), :]
        first_section(left, right, pl.multiple_of(t * half, half))
        return carry

    lax.fori_loop(0, 8, signal_step, 0)
    first_section(
        filter_ref[:, 0:PACK, :].astype(BF16), filter_ref[:, PACK : 2 * PACK, :].astype(BF16), 256
    )

    def spectrum_step(p):
        spec = jnp.dot(twisted_ref[p], forward_ref[...], preferred_element_type=F32)
        filter_r, filter_i = spec[256:288, 0:LANES], spec[256:288, LANES:]
        conv_r, conv_i, back_r, back_i = [], [], [], []
        taps_r = taps_i = None
        for d in range(4):
            at = slice(32 * d, 32 * d + 32)
            value_r, value_i = spec[at, 0:LANES], spec[at, LANES:]
            at = slice(128 + 32 * d, 128 + 32 * d + 32)
            grad_r, grad_i = spec[at, 0:LANES], spec[at, LANES:]
            conv_r.append((value_r * filter_r - value_i * filter_i).astype(BF16))
            conv_i.append((value_r * filter_i + value_i * filter_r).astype(BF16))
            back_r.append((grad_r * filter_r + grad_i * filter_i).astype(BF16))
            back_i.append((grad_i * filter_r - grad_r * filter_i).astype(BF16))
            part_r = grad_r * value_r + grad_i * value_i
            part_i = grad_i * value_r - grad_r * value_i
            taps_r = part_r if d == 0 else taps_r + part_r
            taps_i = part_i if d == 0 else taps_i + part_i
        real = jnp.concatenate(conv_r + back_r + [taps_r.astype(BF16)], axis=0)
        imag = jnp.concatenate(conv_i + back_i + [taps_i.astype(BF16)], axis=0)
        mixture = jnp.dot(
            jnp.concatenate([real, imag], axis=1), inverse_ref[...], preferred_element_type=F32
        )
        first, second = mixture[:, 0:LANES], mixture[:, LANES:]
        at_r = jnp.where(p == half, 1, 2 * p)
        at_i = jnp.where(p == 0, 2 * half, jnp.where(p == half, 2 * half + 1, 2 * p + 1))
        mixed_ref[at_r] = (first * cosine_ref[p] - second * sine_ref[p]).astype(BF16)
        mixed_ref[at_i] = (second * cosine_ref[p] + first * sine_ref[p]).astype(BF16)

    def spectrum_group(n, carry):
        for m in range(3):
            spectrum_step(3 * n + m)
        return carry

    lax.fori_loop(0, (half + 1) // 3, spectrum_group, 0)

    def last_section(row):
        left = mixed_ref[0 : 2 * half, pl.ds(row, PACK), :].reshape(2 * half * PACK, LANES)
        right = mixed_ref[0 : 2 * half, pl.ds(row + PACK, PACK), :].reshape(2 * half * PACK, LANES)
        both = jnp.concatenate([left, right], axis=1)
        return jnp.dot(last_ref[...], both, preferred_element_type=F32)

    def inverse_step(t, carry):
        kind = t // 4
        member = t % 4
        places = pl.ds(pl.multiple_of(member * half, half), half)
        column = pl.multiple_of(kind * half, half)
        result = last_section(pl.multiple_of(t * half, half)).astype(BF16)
        out_ref[places, pl.ds(column, PACK), :] = result[:, 0:LANES].reshape(half, PACK, LANES)
        out_ref[places, pl.ds(column + PACK, PACK), :] = result[:, LANES:].reshape(half, PACK, LANES)
        return carry

    lax.fori_loop(0, 8, inverse_step, 0)
    result = last_section(256)
    filter_ref[:, 0:PACK, :] = result[:, 0:LANES].reshape(half, PACK, LANES)
    filter_ref[:, PACK : 2 * PACK, :] = result[:, LANES:].reshape(half, PACK, LANES)
    pieces = swap_lane_groups([filter_ref[:, 8 * k : 8 * k + 8, :] for k in range(4)])
    stacked = jnp.stack(pieces, axis=1).reshape(4 * half, 8, LANES)
    out_ref[:, 64:72, :] = stacked.astype(BF16)


def on_device(tables, gate_input, values, cotangent, filter_taps):
    channels = values.shape[2]
    peers = lax.axis_size("dp") * lax.axis_size("ctx")
    width = 512
    steps = channels // width
    limit = pltpu.CompilerParams(vmem_limit_bytes=48 * 1024 * 1024)
    wide = pl.BlockSpec((1, LANES, width), lambda n: (0, 0, n))
    taps_block = pl.BlockSpec((32, width), lambda n: (0, n))
    packed_block = pl.BlockSpec((width // 32, 72, LANES), lambda n: (n, 0, 0))
    packed_shape = jax.ShapeDtypeStruct((peers, 72, LANES), BF16)
    packed = pl.pallas_call(
        pack_kernel,
        grid=(steps,),
        in_specs=[wide, wide, wide, taps_block],
        out_specs=packed_block,
        out_shape=packed_shape,
        compiler_params=limit,
        name="pack",
    )(gate_input, values, cotangent, filter_taps)
    received = lax.all_to_all(packed, ("dp", "ctx"), split_axis=0, concat_axis=0, tiled=True)
    whole = pl.BlockSpec(memory_space=pltpu.VMEM)
    results = pl.pallas_call(
        conv_kernel,
        in_specs=[whole] * 7,
        out_specs=whole,
        out_shape=packed_shape,
        scratch_shapes=[
            pltpu.VMEM((32, 32, LANES), F32),
            pltpu.VMEM((33, 288, 2 * LANES), BF16),
            pltpu.VMEM((66, 288, LANES), BF16),
        ],
        compiler_params=limit,
        name="convolve",
    )(received, *tables)
    returned = lax.all_to_all(results, ("dp", "ctx"), split_axis=0, concat_axis=0, tiled=True)
    wide_shape = jax.ShapeDtypeStruct(values.shape, BF16)
    return pl.pallas_call(
        unpack_kernel,
        grid=(steps,),
        in_specs=[wide, wide, packed_block],
        out_specs=[wide, wide, wide, taps_block],
        out_shape=[wide_shape, wide_shape, wide_shape, jax.ShapeDtypeStruct(filter_taps.shape, F32)],
        compiler_params=limit,
        name="unpack",
    )(gate_input, cotangent, returned)


def solution(mesh):
    tables = dft_tables(64)
    specs = (
        P("dp", "ctx", None),
        P("dp", "ctx", None),
        P("dp", "ctx", None),
        P(("dp", "ctx"), None),
    )

    def program(gate_input, values, cotangent, filter_taps):
        body = functools.partial(on_device, tables)
        return jax.shard_map(
            lambda *args: tuple(body(*args)), mesh=mesh, in_specs=specs, out_specs=specs, check_vma=False
        )(gate_input, values, cotangent, filter_taps)

    return program
```

```python
import functools
import math

import jax
import jax.numpy as jnp
import ml_dtypes
import numpy as np
from jax import lax
from jax.experimental import pallas as pl
from jax.experimental.pallas import tpu as pltpu
from jax.sharding import PartitionSpec as P

LANES = 128
PACK = 16
PACK_LIMIT = 16 * 1024 * 1024
CONV_LIMIT = 32 * 1024 * 1024
BF16 = jnp.bfloat16
F32 = jnp.float32


def angle_tables(top, bottom, period):
    angles = (np.outer(top, bottom) % period).astype(np.float64) * (2.0 * math.pi / period)
    return np.cos(angles).astype(np.float32), np.sin(angles).astype(np.float32)


def block_diagonal(table):
    eye = np.eye(PACK, dtype=np.float32)
    return np.kron(table, eye).astype(ml_dtypes.bfloat16)


def dft_tables(blocks):
    freq_len = blocks * LANES
    half = blocks // 2
    quarter = half // 2
    firsts, lasts = [], []
    for parity in range(2):
        places = np.arange(parity, half, 2)
        cosine, sine = angle_tables(np.arange(quarter + 1), places, blocks)
        base = np.zeros((half, quarter), np.float32)
        base[0] = cosine[0]
        base[1] = cosine[quarter] if parity == 0 else -sine[quarter]
        for p in range(1, quarter):
            base[2 * p] = cosine[p]
            base[2 * p + 1] = -sine[p]
        weight = np.full((half, 1), 2.0 / freq_len, np.float32)
        weight[0] = 1.0 / freq_len
        firsts.append(block_diagonal(base))
        lasts.append(block_diagonal((base * weight).T))
    order = [p for u in range(quarter) for p in (u, half - u)] + [quarter]
    twist_cosine, twist_sine = angle_tables(np.array(order), np.arange(LANES), freq_len)
    inner_cosine, inner_sine = angle_tables(np.arange(LANES), np.arange(LANES), LANES)
    forward = np.block([[inner_cosine, -inner_sine], [inner_sine, inner_cosine]])
    inverse = np.block([[inner_cosine, inner_sine], [-inner_sine, inner_cosine]])
    return (
        np.stack(firsts),
        np.stack(lasts),
        twist_cosine[:, None, :],
        twist_sine[:, None, :],
        forward.astype(ml_dtypes.bfloat16),
        inverse.astype(ml_dtypes.bfloat16),
    )


def swap_lane_groups(pieces):
    count = len(pieces)
    width = LANES // count
    group = lax.broadcasted_iota(jnp.int32, pieces[0].shape, pieces[0].ndim - 1) // width
    results = []
    for g in range(count):
        total = None
        for k in range(count):
            shift = (width * (k - g)) % LANES
            moved = pieces[k] if shift == 0 else pltpu.roll(pieces[k], shift, pieces[k].ndim - 1)
            total = moved if total is None else jnp.where(group == k, moved, total)
        results.append(total)
    return results


def in_place(array):
    return pltpu.with_memory_space_constraint(array, pltpu.HBM)


def pack_kernel(
    gate_any, values_any, cotangent_any, taps_any, packed_ref,
    gate_ref, values_ref, cotangent_ref, taps_ref, arrived,
):
    pairs = (
        (values_any, values_ref),
        (cotangent_any, cotangent_ref),
        (gate_any, gate_ref),
        (taps_any, taps_ref),
    )
    chunks = arrived.shape[1]
    columns = taps_ref.shape[-1] // chunks
    per_peer = 32
    peers = columns // per_peer

    def copy(n, m):
        source, target = pairs[m]
        at = slice(n * columns, (n + 1) * columns)
        if m == 3:
            return pltpu.make_async_copy(source.at[:, at], target.at[:, at], arrived.at[m, n])
        return pltpu.make_async_copy(source.at[0, :, at], target.at[:, at], arrived.at[m, n])

    for n in range(chunks):
        for m in range(4):
            copy(n, m).start()
    for n in range(chunks):
        at = slice(n * columns, (n + 1) * columns)
        to = slice(n * peers, (n + 1) * peers)
        copy(n, 0).wait()
        packed_ref[to, 0:per_peer, :] = values_ref[:, at].T.reshape(peers, per_peer, LANES)
        copy(n, 1).wait()
        copy(n, 2).wait()
        grad = (cotangent_ref[:, at].astype(F32) * gate_ref[:, at].astype(F32)).astype(BF16)
        packed_ref[to, per_peer : 2 * per_peer, :] = grad.T.reshape(peers, per_peer, LANES)
        copy(n, 3).wait()
        taps = taps_ref[:, at]
        for block in range(columns // 512):
            start = 512 * block
            stacked = jnp.concatenate(
                [taps[:, start + LANES * i : start + LANES * (i + 1)] for i in range(4)], axis=0
            )
            turned = stacked.T.reshape(4, 4, 8, LANES)
            pieces = swap_lane_groups([turned[:, k] for k in range(4)])
            for i in range(4):
                first = n * peers + 16 * block + 4 * i
                packed_ref[first : first + 4, 2 * per_peer : 2 * per_peer + 8, :] = pieces[i].astype(BF16)


def pack(gate_input, values, cotangent, filter_taps):
    channels = values.shape[2]
    chunks = 4
    anywhere = pl.BlockSpec(memory_space=pltpu.HBM)
    return pl.pallas_call(
        pack_kernel,
        in_specs=[anywhere] * 4,
        out_specs=pl.BlockSpec(memory_space=pltpu.VMEM),
        out_shape=jax.ShapeDtypeStruct((channels // 32, 72, LANES), BF16),
        scratch_shapes=[
            pltpu.VMEM((LANES, channels), BF16),
            pltpu.VMEM((LANES, channels), BF16),
            pltpu.VMEM((LANES, channels), BF16),
            pltpu.VMEM((32, channels), F32),
            pltpu.SemaphoreType.DMA((4, chunks)),
        ],
        compiler_params=pltpu.CompilerParams(vmem_limit_bytes=PACK_LIMIT),
        name="pack",
    )(*[in_place(x) for x in (gate_input, values, cotangent, filter_taps)])


def unpack_kernel(
    gate_any, cotangent_any, packed_ref, output_any, gate_grad_any, values_grad_any, taps_any,
    gate_ref, cotangent_ref, output_ref, gate_grad_ref, values_grad_ref, taps_ref, arrived, left,
):
    pairs = (
        (values_grad_ref, values_grad_any),
        (output_ref, output_any),
        (gate_grad_ref, gate_grad_any),
        (taps_ref, taps_any),
    )
    chunks = left.shape[1]
    columns = taps_ref.shape[-1] // chunks
    per_peer = 32
    peers = columns // per_peer

    def copy(n, m):
        source, target = pairs[m]
        at = slice(n * columns, (n + 1) * columns)
        if m == 3:
            return pltpu.make_async_copy(source.at[:, at], target.at[:, at], left.at[m, n])
        return pltpu.make_async_copy(source.at[:, at], target.at[0, :, at], left.at[m, n])

    def fetch(n, m):
        at = slice(n * columns, (n + 1) * columns)
        source, target = ((gate_any, gate_ref), (cotangent_any, cotangent_ref))[m]
        return pltpu.make_async_copy(source.at[0, :, at], target.at[:, at], arrived.at[m, n])

    for n in range(chunks):
        for m in range(2):
            fetch(n, m).start()
    for n in range(chunks):
        at = slice(n * columns, (n + 1) * columns)
        of = slice(n * peers, (n + 1) * peers)
        values_grad_ref[:, at] = packed_ref[of, per_peer : 2 * per_peer, :].reshape(columns, LANES).T
        copy(n, 0).start()
        taps = packed_ref[of, 2 * per_peer : 2 * per_peer + 8, :].astype(F32)
        for block in range(columns // 512):
            pieces = swap_lane_groups(
                [taps[16 * block + 4 * i : 16 * block + 4 * i + 4] for i in range(4)]
            )
            stacked = jnp.stack(pieces, axis=1).reshape(LANES, LANES).T
            for i in range(4):
                start = n * columns + 512 * block + LANES * i
                taps_ref[:, start : start + LANES] = stacked[32 * i : 32 * i + 32, :]
        copy(n, 3).start()
    for n in range(chunks):
        at = slice(n * columns, (n + 1) * columns)
        of = slice(n * peers, (n + 1) * peers)
        conv = packed_ref[of, 0:per_peer, :].reshape(columns, LANES).T.astype(F32)
        fetch(n, 0).wait()
        output_ref[:, at] = (gate_ref[:, at].astype(F32) * conv).astype(BF16)
        copy(n, 1).start()
        fetch(n, 1).wait()
        gate_grad_ref[:, at] = (cotangent_ref[:, at].astype(F32) * conv).astype(BF16)
        copy(n, 2).start()
    for n in range(chunks):
        for m in range(4):
            copy(n, m).wait()


def unpack(gate_input, cotangent, packed):
    channels = gate_input.shape[2]
    chunks = 4
    within = pl.BlockSpec(memory_space=pltpu.VMEM)
    outside = pl.BlockSpec(memory_space=pltpu.HBM)
    wide_shape = jax.ShapeDtypeStruct(gate_input.shape, BF16)
    return pl.pallas_call(
        unpack_kernel,
        in_specs=[outside, outside, within],
        out_specs=[outside] * 4,
        out_shape=[wide_shape, wide_shape, wide_shape, jax.ShapeDtypeStruct((32, channels), F32)],
        scratch_shapes=[
            pltpu.VMEM((LANES, channels), BF16),
            pltpu.VMEM((LANES, channels), BF16),
            pltpu.VMEM((LANES, channels), BF16),
            pltpu.VMEM((LANES, channels), BF16),
            pltpu.VMEM((LANES, channels), BF16),
            pltpu.VMEM((32, channels), F32),
            pltpu.SemaphoreType.DMA((2, chunks)),
            pltpu.SemaphoreType.DMA((4, chunks)),
        ],
        compiler_params=pltpu.CompilerParams(vmem_limit_bytes=PACK_LIMIT),
        name="unpack",
    )(in_place(gate_input), in_place(cotangent), packed)


def conv_kernel(
    data_ref, first_ref, last_ref, cosine_ref, sine_ref, forward_ref, inverse_ref, out_ref,
    filter_ref, twisted_ref, mixed_ref,
):
    half = 32
    quarter = 16
    rows = 288

    taps = data_ref[:, 64:72, :].astype(F32).reshape(half, 4, 8, LANES)
    pieces = swap_lane_groups([taps[:, m] for m in range(4)])
    for k in range(4):
        filter_ref[:, 8 * k : 8 * k + 8, :] = pieces[k]

    def put_twisted(at, target, real, imag):
        cosine, sine = cosine_ref[at], sine_ref[at]
        twisted_ref[at, target, 0:LANES] = (real * cosine + imag * sine).astype(BF16)
        twisted_ref[at, target, LANES : 2 * LANES] = (imag * cosine - real * sine).astype(BF16)

    def first_section(left, right, row):
        def parity_rows(parity):
            sides = [
                side.reshape(quarter, 2, PACK, LANES)[:, parity].reshape(quarter * PACK, LANES)
                for side in (left, right)
            ]
            return jnp.dot(
                first_ref[parity], jnp.concatenate(sides, axis=1), preferred_element_type=F32
            )

        even, odd = parity_rows(0), parity_rows(1)
        for side in range(2):
            lanes = slice(LANES * side, LANES * (side + 1))
            target = slice(row + PACK * side, row + PACK * side + PACK)
            even_0, odd_0 = even[0:PACK, lanes], odd[0:PACK, lanes]
            twisted_ref[0, target, 0:LANES] = (even_0 + odd_0).astype(BF16)
            twisted_ref[0, target, LANES : 2 * LANES] = jnp.zeros((PACK, LANES), BF16)
            part = even_0 - odd_0
            twisted_ref[1, target, 0:LANES] = (part * cosine_ref[1]).astype(BF16)
            twisted_ref[1, target, LANES : 2 * LANES] = (-part * sine_ref[1]).astype(BF16)
            put_twisted(half, target, even[PACK : 2 * PACK, lanes], odd[PACK : 2 * PACK, lanes])
            for u in range(1, quarter):
                at_r = slice(2 * u * PACK, (2 * u + 1) * PACK)
                at_i = slice((2 * u + 1) * PACK, (2 * u + 2) * PACK)
                even_r, even_i = even[at_r, lanes], even[at_i, lanes]
                odd_r, odd_i = odd[at_r, lanes], odd[at_i, lanes]
                put_twisted(2 * u, target, even_r + odd_r, even_i + odd_i)
                put_twisted(2 * u + 1, target, even_r - odd_r, odd_i - even_i)

    def places_of(t):
        member = t % 4
        column = (t // 4) * half
        return slice(member * half, member * half + half), column

    for t in range(8):
        places, column = places_of(t)
        left = data_ref[places, column : column + PACK, :]
        right = data_ref[places, column + PACK : column + 2 * PACK, :]
        first_section(left, right, t * half)
    first_section(
        filter_ref[:, 0:PACK, :].astype(BF16), filter_ref[:, PACK : 2 * PACK, :].astype(BF16), 256
    )

    def products(spec):
        filter_r, filter_i = spec[256:288, 0:LANES], spec[256:288, LANES:]
        conv_r, conv_i, back_r, back_i = [], [], [], []
        taps_r = taps_i = None
        for d in range(4):
            at = slice(32 * d, 32 * d + 32)
            value_r, value_i = spec[at, 0:LANES], spec[at, LANES:]
            at = slice(128 + 32 * d, 128 + 32 * d + 32)
            grad_r, grad_i = spec[at, 0:LANES], spec[at, LANES:]
            conv_r.append((value_r * filter_r - value_i * filter_i).astype(BF16))
            conv_i.append((value_r * filter_i + value_i * filter_r).astype(BF16))
            back_r.append((grad_r * filter_r + grad_i * filter_i).astype(BF16))
            back_i.append((grad_i * filter_r - grad_r * filter_i).astype(BF16))
            part_r = grad_r * value_r + grad_i * value_i
            part_i = grad_i * value_r - grad_r * value_i
            taps_r = part_r if d == 0 else taps_r + part_r
            taps_i = part_i if d == 0 else taps_i + part_i
        real = jnp.concatenate(conv_r + back_r + [taps_r.astype(BF16)], axis=0)
        imag = jnp.concatenate(conv_i + back_i + [taps_i.astype(BF16)], axis=0)
        return jnp.concatenate([real, imag], axis=1)

    def spectra(start, count):
        block = twisted_ref[start : start + count].reshape(count * rows, 2 * LANES)
        spec = jnp.dot(block, forward_ref[...], preferred_element_type=F32)
        mixed = jnp.concatenate(
            [products(spec[rows * j : rows * (j + 1)]) for j in range(count)], axis=0
        )
        mixture = jnp.dot(mixed, inverse_ref[...], preferred_element_type=F32)
        results = []
        for j in range(count):
            at = slice(rows * j, rows * (j + 1))
            first, second = mixture[at, 0:LANES], mixture[at, LANES:]
            cosine, sine = cosine_ref[start + j], sine_ref[start + j]
            results.append((first * cosine - second * sine, second * cosine + first * sine))
        return results

    ((middle_r, middle_i),) = spectra(half, 1)
    mixed_ref[0, 1] = middle_r.astype(BF16)
    mixed_ref[1, 1] = middle_i.astype(BF16)
    for u in range(quarter):
        (low_r, low_i), (high_r, high_i) = spectra(2 * u, 2)
        mixed_ref[0, 2 * u] = (low_r + high_r).astype(BF16)
        mixed_ref[1, 2 * u] = (low_r - high_r).astype(BF16)
        if u > 0:
            mixed_ref[0, 2 * u + 1] = (low_i - high_i).astype(BF16)
            mixed_ref[1, 2 * u + 1] = (low_i + high_i).astype(BF16)

    def last_section(row):
        results = []
        for parity in range(2):
            sides = [
                mixed_ref[parity, :, row + PACK * side : row + PACK * side + PACK, :].reshape(half * PACK, LANES)
                for side in range(2)
            ]
            part = jnp.dot(
                last_ref[parity], jnp.concatenate(sides, axis=1), preferred_element_type=F32
            )
            results.append(part.reshape(quarter, PACK, 2 * LANES))
        whole = jnp.stack(results, axis=1).reshape(half, PACK, 2 * LANES)
        return whole[:, :, 0:LANES], whole[:, :, LANES:]

    left, right = last_section(256)
    filter_ref[:, 0:PACK, :] = left
    filter_ref[:, PACK : 2 * PACK, :] = right
    pieces = swap_lane_groups([filter_ref[:, 8 * k : 8 * k + 8, :] for k in range(4)])
    stacked = jnp.stack(pieces, axis=1).reshape(4 * half, 8, LANES)
    out_ref[:, 64:72, :] = stacked.astype(BF16)
    for t in range(8):
        places, column = places_of(t)
        left, right = last_section(t * half)
        out_ref[places, column : column + PACK, :] = left.astype(BF16)
        out_ref[places, column + PACK : column + 2 * PACK, :] = right.astype(BF16)


def convolve(received, tables):
    whole = pl.BlockSpec(memory_space=pltpu.VMEM)
    return pl.pallas_call(
        conv_kernel,
        in_specs=[whole] * 7,
        out_specs=whole,
        out_shape=jax.ShapeDtypeStruct(received.shape, BF16),
        scratch_shapes=[
            pltpu.VMEM((32, 32, LANES), F32),
            pltpu.VMEM((33, 288, 2 * LANES), BF16),
            pltpu.VMEM((2, 32, 288, LANES), BF16),
        ],
        compiler_params=pltpu.CompilerParams(vmem_limit_bytes=CONV_LIMIT),
        name="convolve",
    )(received, *tables)


def exchange(blocks):
    return lax.all_to_all(blocks, ("dp", "ctx"), split_axis=0, concat_axis=0, tiled=True)


def on_device(tables, gate_input, values, cotangent, filter_taps):
    received = exchange(pack(gate_input, values, cotangent, filter_taps))
    returned = exchange(convolve(received, tables))
    return unpack(gate_input, cotangent, returned)


def solution(mesh):
    tables = dft_tables(64)
    specs = (
        P("dp", "ctx", None),
        P("dp", "ctx", None),
        P("dp", "ctx", None),
        P(("dp", "ctx"), None),
    )

    def program(gate_input, values, cotangent, filter_taps):
        body = functools.partial(on_device, tables)
        return jax.shard_map(
            lambda *args: tuple(body(*args)), mesh=mesh, in_specs=specs, out_specs=specs, check_vma=False
        )(*[in_place(x) for x in (gate_input, values, cotangent, filter_taps)])

    return program
```

```python
import functools
import math

import jax
import jax.numpy as jnp
import ml_dtypes
import numpy as np
from jax import lax
from jax.experimental import pallas as pl
from jax.experimental.pallas import tpu as pltpu
from jax.sharding import PartitionSpec as P

LANES = 128
PACK = 16
PACK_CHUNKS = 4
UNPACK_CHUNKS = 4
PACK_LIMIT = 16 * 1024 * 1024
CONV_LIMIT = 32 * 1024 * 1024
BF16 = jnp.bfloat16
F32 = jnp.float32


def angle_tables(top, bottom, period):
    angles = (np.outer(top, bottom) % period).astype(np.float64) * (2.0 * math.pi / period)
    return np.cos(angles).astype(np.float32), np.sin(angles).astype(np.float32)


def block_diagonal(table):
    eye = np.eye(PACK, dtype=np.float32)
    return np.kron(table, eye).astype(ml_dtypes.bfloat16)


def dft_tables(blocks):
    freq_len = blocks * LANES
    half = blocks // 2
    quarter = half // 2
    firsts, lasts = [], []
    for parity in range(2):
        places = np.arange(parity, half, 2)
        cosine, sine = angle_tables(np.arange(quarter + 1), places, blocks)
        base = np.zeros((half, quarter), np.float32)
        base[0] = cosine[0]
        base[1] = cosine[quarter] if parity == 0 else -sine[quarter]
        for p in range(1, quarter):
            base[2 * p] = cosine[p]
            base[2 * p + 1] = -sine[p]
        weight = np.full((half, 1), 2.0 / freq_len, np.float32)
        weight[0] = 1.0 / freq_len
        firsts.append(block_diagonal(base))
        lasts.append(block_diagonal((base * weight).T))
    order = [p for u in range(quarter) for p in (u, half - u)] + [quarter]
    twist_cosine, twist_sine = angle_tables(np.array(order), np.arange(LANES), freq_len)
    inner_cosine, inner_sine = angle_tables(np.arange(LANES), np.arange(LANES), LANES)
    forward = np.block([[inner_cosine, -inner_sine], [inner_sine, inner_cosine]])
    inverse = np.block([[inner_cosine, inner_sine], [-inner_sine, inner_cosine]])
    return (
        np.stack(firsts),
        np.stack(lasts),
        twist_cosine[:, None, :],
        twist_sine[:, None, :],
        forward.astype(ml_dtypes.bfloat16),
        inverse.astype(ml_dtypes.bfloat16),
    )


def swap_lane_groups(pieces):
    count = len(pieces)
    width = LANES // count
    group = lax.broadcasted_iota(jnp.int32, pieces[0].shape, pieces[0].ndim - 1) // width
    results = []
    for g in range(count):
        total = None
        for k in range(count):
            shift = (width * (k - g)) % LANES
            moved = pieces[k] if shift == 0 else pltpu.roll(pieces[k], shift, pieces[k].ndim - 1)
            total = moved if total is None else jnp.where(group == k, moved, total)
        results.append(total)
    return results


def in_place(array):
    return pltpu.with_memory_space_constraint(array, pltpu.HBM)


def pack_kernel(
    gate_any, values_any, cotangent_any, taps_any, packed_ref, gate_ref, cotangent_ref,
    values_ref, taps_ref, arrived,
):
    pairs = (
        (values_any, values_ref),
        (cotangent_any, cotangent_ref),
        (gate_any, gate_ref),
        (taps_any, taps_ref),
    )
    chunks = arrived.shape[1]
    columns = taps_ref.shape[-1] // chunks
    per_peer = 32
    peers = columns // per_peer

    def copy(n, m):
        source, target = pairs[m]
        at = slice(n * columns, (n + 1) * columns)
        if m == 3:
            return pltpu.make_async_copy(source.at[:, at], target.at[:, at], arrived.at[m, n])
        return pltpu.make_async_copy(source.at[0, :, at], target.at[:, at], arrived.at[m, n])

    for n in range(chunks):
        for m in range(4):
            copy(n, m).start()
    for n in range(chunks):
        at = slice(n * columns, (n + 1) * columns)
        to = slice(n * peers, (n + 1) * peers)
        copy(n, 0).wait()
        packed_ref[to, 0:per_peer, :] = values_ref[:, at].T.reshape(peers, per_peer, LANES)
        copy(n, 1).wait()
        copy(n, 2).wait()
        grad = (cotangent_ref[:, at].astype(F32) * gate_ref[:, at].astype(F32)).astype(BF16)
        packed_ref[to, per_peer : 2 * per_peer, :] = grad.T.reshape(peers, per_peer, LANES)
        copy(n, 3).wait()
        taps = taps_ref[:, at]
        for block in range(columns // 512):
            start = 512 * block
            stacked = jnp.concatenate(
                [taps[:, start + LANES * i : start + LANES * (i + 1)] for i in range(4)], axis=0
            )
            turned = stacked.T.reshape(4, 4, 8, LANES)
            pieces = swap_lane_groups([turned[:, k] for k in range(4)])
            for i in range(4):
                first = n * peers + 16 * block + 4 * i
                packed_ref[first : first + 4, 2 * per_peer : 2 * per_peer + 8, :] = pieces[i].astype(BF16)


def pack(gate_input, values, cotangent, filter_taps):
    channels = values.shape[2]
    chunks = PACK_CHUNKS
    anywhere = pl.BlockSpec(memory_space=pltpu.HBM)
    return pl.pallas_call(
        pack_kernel,
        in_specs=[anywhere] * 4,
        out_specs=[pl.BlockSpec(memory_space=pltpu.VMEM)] * 3,
        out_shape=[
            jax.ShapeDtypeStruct((channels // 32, 72, LANES), BF16),
            jax.ShapeDtypeStruct((LANES, channels), BF16),
            jax.ShapeDtypeStruct((LANES, channels), BF16),
        ],
        scratch_shapes=[
            pltpu.VMEM((LANES, channels), BF16),
            pltpu.VMEM((32, channels), F32),
            pltpu.SemaphoreType.DMA((4, chunks)),
        ],
        compiler_params=pltpu.CompilerParams(vmem_limit_bytes=PACK_LIMIT),
        name="pack",
    )(*[in_place(x) for x in (gate_input, values, cotangent, filter_taps)])


def unpack_kernel(
    gate_ref, cotangent_ref, packed_ref, output_any, gate_grad_any, values_grad_any, taps_any,
    output_ref, gate_grad_ref, values_grad_ref, taps_ref, left,
):
    pairs = (
        (values_grad_ref, values_grad_any),
        (output_ref, output_any),
        (gate_grad_ref, gate_grad_any),
        (taps_ref, taps_any),
    )
    chunks = left.shape[1]
    columns = taps_ref.shape[-1] // chunks
    per_peer = 32
    peers = columns // per_peer

    def copy(n, m):
        source, target = pairs[m]
        at = slice(n * columns, (n + 1) * columns)
        if m == 3:
            return pltpu.make_async_copy(source.at[:, at], target.at[:, at], left.at[m, n])
        return pltpu.make_async_copy(source.at[:, at], target.at[0, :, at], left.at[m, n])

    for n in range(chunks):
        at = slice(n * columns, (n + 1) * columns)
        of = slice(n * peers, (n + 1) * peers)
        values_grad_ref[:, at] = packed_ref[of, per_peer : 2 * per_peer, :].reshape(columns, LANES).T
        copy(n, 0).start()
        conv = packed_ref[of, 0:per_peer, :].reshape(columns, LANES).T.astype(F32)
        output_ref[:, at] = (gate_ref[:, at].astype(F32) * conv).astype(BF16)
        copy(n, 1).start()
        gate_grad_ref[:, at] = (cotangent_ref[:, at].astype(F32) * conv).astype(BF16)
        copy(n, 2).start()
        taps = packed_ref[of, 2 * per_peer : 2 * per_peer + 8, :].astype(F32)
        for block in range(columns // 512):
            pieces = swap_lane_groups(
                [taps[16 * block + 4 * i : 16 * block + 4 * i + 4] for i in range(4)]
            )
            stacked = jnp.stack(pieces, axis=1).reshape(LANES, LANES).T
            for i in range(4):
                start = n * columns + 512 * block + LANES * i
                taps_ref[:, start : start + LANES] = stacked[32 * i : 32 * i + 32, :]
        copy(n, 3).start()
    for n in range(chunks):
        for m in range(4):
            copy(n, m).wait()


def unpack(gate_input, cotangent, packed):
    channels = gate_input.shape[1]
    chunks = UNPACK_CHUNKS
    within = pl.BlockSpec(memory_space=pltpu.VMEM)
    outside = pl.BlockSpec(memory_space=pltpu.HBM)
    wide_shape = jax.ShapeDtypeStruct((1, LANES, channels), BF16)
    return pl.pallas_call(
        unpack_kernel,
        in_specs=[within] * 3,
        out_specs=[outside] * 4,
        out_shape=[wide_shape, wide_shape, wide_shape, jax.ShapeDtypeStruct((32, channels), F32)],
        scratch_shapes=[
            pltpu.VMEM((LANES, channels), BF16),
            pltpu.VMEM((LANES, channels), BF16),
            pltpu.VMEM((LANES, channels), BF16),
            pltpu.VMEM((32, channels), F32),
            pltpu.SemaphoreType.DMA((4, chunks)),
        ],
        compiler_params=pltpu.CompilerParams(vmem_limit_bytes=PACK_LIMIT),
        name="unpack",
    )(gate_input, cotangent, packed)


def conv_kernel(
    data_ref, first_ref, last_ref, cosine_ref, sine_ref, forward_ref, inverse_ref, out_ref,
    filter_ref, twisted_ref, mixed_ref,
):
    half = 32
    quarter = 16
    rows = 288

    taps = data_ref[:, :, 64:72, :].astype(F32).reshape(8, 4, 4, 8, LANES)
    pieces = swap_lane_groups(
        [jnp.concatenate([taps[:, m, d] for d in range(4)], axis=0) for m in range(4)]
    )
    for k in range(4):
        filter_ref[:, 8 * k : 8 * k + 8, :] = pieces[k]

    def put_twisted(at, target, real, imag):
        cosine, sine = cosine_ref[at], sine_ref[at]
        twisted_ref[at, target, 0:LANES] = (real * cosine + imag * sine).astype(BF16)
        twisted_ref[at, target, LANES : 2 * LANES] = (imag * cosine - real * sine).astype(BF16)

    def first_section(left, right, row):
        def parity_rows(parity):
            sides = [
                side.reshape(quarter, 2, PACK, LANES)[:, parity].reshape(quarter * PACK, LANES)
                for side in (left, right)
            ]
            return jnp.dot(
                first_ref[parity], jnp.concatenate(sides, axis=1), preferred_element_type=F32
            )

        even, odd = parity_rows(0), parity_rows(1)
        for side in range(2):
            lanes = slice(LANES * side, LANES * (side + 1))
            target = slice(row + PACK * side, row + PACK * side + PACK)
            even_0, odd_0 = even[0:PACK, lanes], odd[0:PACK, lanes]
            twisted_ref[0, target, 0:LANES] = (even_0 + odd_0).astype(BF16)
            twisted_ref[0, target, LANES : 2 * LANES] = jnp.zeros((PACK, LANES), BF16)
            part = even_0 - odd_0
            twisted_ref[1, target, 0:LANES] = (part * cosine_ref[1]).astype(BF16)
            twisted_ref[1, target, LANES : 2 * LANES] = (-part * sine_ref[1]).astype(BF16)
            put_twisted(half, target, even[PACK : 2 * PACK, lanes], odd[PACK : 2 * PACK, lanes])
            for u in range(1, quarter):
                at_r = slice(2 * u * PACK, (2 * u + 1) * PACK)
                at_i = slice((2 * u + 1) * PACK, (2 * u + 2) * PACK)
                even_r, even_i = even[at_r, lanes], even[at_i, lanes]
                odd_r, odd_i = odd[at_r, lanes], odd[at_i, lanes]
                put_twisted(2 * u, target, even_r + odd_r, even_i + odd_i)
                put_twisted(2 * u + 1, target, even_r - odd_r, odd_i - even_i)

    for t in range(8):
        column = (t // 4) * half
        left = data_ref[:, t % 4, column : column + PACK, :]
        right = data_ref[:, t % 4, column + PACK : column + 2 * PACK, :]
        first_section(left, right, t * half)
    first_section(
        filter_ref[:, 0:PACK, :].astype(BF16), filter_ref[:, PACK : 2 * PACK, :].astype(BF16), 256
    )

    def products(spec):
        filter_r, filter_i = spec[256:288, 0:LANES], spec[256:288, LANES:]
        conv_r, conv_i, back_r, back_i = [], [], [], []
        taps_r = taps_i = None
        for d in range(4):
            at = slice(32 * d, 32 * d + 32)
            value_r, value_i = spec[at, 0:LANES], spec[at, LANES:]
            at = slice(128 + 32 * d, 128 + 32 * d + 32)
            grad_r, grad_i = spec[at, 0:LANES], spec[at, LANES:]
            conv_r.append((value_r * filter_r - value_i * filter_i).astype(BF16))
            conv_i.append((value_r * filter_i + value_i * filter_r).astype(BF16))
            back_r.append((grad_r * filter_r + grad_i * filter_i).astype(BF16))
            back_i.append((grad_i * filter_r - grad_r * filter_i).astype(BF16))
            part_r = grad_r * value_r + grad_i * value_i
            part_i = grad_i * value_r - grad_r * value_i
            taps_r = part_r if d == 0 else taps_r + part_r
            taps_i = part_i if d == 0 else taps_i + part_i
        real = jnp.concatenate(conv_r + back_r + [taps_r.astype(BF16)], axis=0)
        imag = jnp.concatenate(conv_i + back_i + [taps_i.astype(BF16)], axis=0)
        return jnp.concatenate([real, imag], axis=1)

    def spectra(start, count):
        block = twisted_ref[start : start + count].reshape(count * rows, 2 * LANES)
        spec = jnp.dot(block, forward_ref[...], preferred_element_type=F32)
        mixed = jnp.concatenate(
            [products(spec[rows * j : rows * (j + 1)]) for j in range(count)], axis=0
        )
        mixture = jnp.dot(mixed, inverse_ref[...], preferred_element_type=F32)
        results = []
        for j in range(count):
            at = slice(rows * j, rows * (j + 1))
            first, second = mixture[at, 0:LANES], mixture[at, LANES:]
            cosine, sine = cosine_ref[start + j], sine_ref[start + j]
            results.append((first * cosine - second * sine, second * cosine + first * sine))
        return results

    ((middle_r, middle_i),) = spectra(half, 1)
    mixed_ref[0, 1] = middle_r.astype(BF16)
    mixed_ref[1, 1] = middle_i.astype(BF16)
    for u in range(quarter):
        (low_r, low_i), (high_r, high_i) = spectra(2 * u, 2)
        mixed_ref[0, 2 * u] = (low_r + high_r).astype(BF16)
        mixed_ref[1, 2 * u] = (low_r - high_r).astype(BF16)
        if u > 0:
            mixed_ref[0, 2 * u + 1] = (low_i - high_i).astype(BF16)
            mixed_ref[1, 2 * u + 1] = (low_i + high_i).astype(BF16)

    def last_section(row):
        results = []
        for parity in range(2):
            sides = [
                mixed_ref[parity, :, row + PACK * side : row + PACK * side + PACK, :].reshape(half * PACK, LANES)
                for side in range(2)
            ]
            part = jnp.dot(
                last_ref[parity], jnp.concatenate(sides, axis=1), preferred_element_type=F32
            )
            results.append(part.reshape(quarter, PACK, 2 * LANES))
        whole = jnp.stack(results, axis=1).reshape(half, PACK, 2 * LANES)
        return whole[:, :, 0:LANES], whole[:, :, LANES:]

    left, right = last_section(256)
    filter_ref[:, 0:PACK, :] = left
    filter_ref[:, PACK : 2 * PACK, :] = right
    pieces = swap_lane_groups([filter_ref[:, 8 * k : 8 * k + 8, :] for k in range(4)])
    for m in range(4):
        for d in range(4):
            part = pieces[m][8 * d : 8 * d + 8].astype(BF16)
            for high in range(8):
                out_ref[4 * high + m, d, 64:72, :] = part[high]
    for t in range(8):
        column = (t // 4) * half
        left, right = last_section(t * half)
        out_ref[:, t % 4, column : column + PACK, :] = left.astype(BF16)
        out_ref[:, t % 4, column + PACK : column + 2 * PACK, :] = right.astype(BF16)


def convolve(received, tables):
    whole = pl.BlockSpec(memory_space=pltpu.VMEM)
    return pl.pallas_call(
        conv_kernel,
        in_specs=[whole] * 7,
        out_specs=whole,
        out_shape=jax.ShapeDtypeStruct(received.shape, BF16),
        scratch_shapes=[
            pltpu.VMEM((32, 32, LANES), F32),
            pltpu.VMEM((33, 288, 2 * LANES), BF16),
            pltpu.VMEM((2, 32, 288, LANES), BF16),
        ],
        compiler_params=pltpu.CompilerParams(vmem_limit_bytes=CONV_LIMIT),
        name="convolve",
    )(received, *tables)


def exchange(blocks):
    return lax.all_to_all(blocks, ("ctx", "dp"), split_axis=0, concat_axis=0, tiled=True)


def on_device(tables, gate_input, values, cotangent, filter_taps):
    packed, gate_held, cotangent_held = pack(gate_input, values, cotangent, filter_taps)
    by_member = (lax.axis_size("ctx"), lax.axis_size("dp")) + packed.shape[1:]
    results = convolve(exchange(packed).reshape(by_member), tables)
    returned = exchange(results.reshape(packed.shape))
    return unpack(gate_held, cotangent_held, returned)


def solution(mesh):
    tables = dft_tables(64)
    specs = (
        P("dp", "ctx", None),
        P("dp", "ctx", None),
        P("dp", "ctx", None),
        P(("dp", "ctx"), None),
    )

    def program(gate_input, values, cotangent, filter_taps):
        body = functools.partial(on_device, tables)
        return jax.shard_map(
            lambda *args: tuple(body(*args)), mesh=mesh, in_specs=specs, out_specs=specs, check_vma=False
        )(*[in_place(x) for x in (gate_input, values, cotangent, filter_taps)])

    return program
```

```python
import functools
import math

import jax
import jax.numpy as jnp
import ml_dtypes
import numpy as np
from jax import lax
from jax.experimental import pallas as pl
from jax.experimental.pallas import tpu as pltpu
from jax.sharding import PartitionSpec as P

LANES = 128
PACK = 16
PACK_CHUNKS = 4
UNPACK_CHUNKS = 4
PACK_LIMIT = 16 * 1024 * 1024
CONV_LIMIT = 32 * 1024 * 1024
BF16 = jnp.bfloat16
F32 = jnp.float32


def angle_tables(top, bottom, period):
    angles = (np.outer(top, bottom) % period).astype(np.float64) * (2.0 * math.pi / period)
    return np.cos(angles).astype(np.float32), np.sin(angles).astype(np.float32)


def block_diagonal(table):
    eye = np.eye(PACK, dtype=np.float32)
    return np.kron(table, eye).astype(ml_dtypes.bfloat16)


def dft_tables(blocks):
    freq_len = blocks * LANES
    half = blocks // 2
    quarter = half // 2
    firsts, lasts = [], []
    for parity in range(2):
        places = np.arange(parity, half, 2)
        cosine, sine = angle_tables(np.arange(quarter + 1), places, blocks)
        base = np.zeros((half, quarter), np.float32)
        base[0] = cosine[0]
        base[1] = cosine[quarter] if parity == 0 else -sine[quarter]
        for p in range(1, quarter):
            base[2 * p] = cosine[p]
            base[2 * p + 1] = -sine[p]
        weight = np.full((half, 1), 2.0 / freq_len, np.float32)
        weight[0] = 1.0 / freq_len
        firsts.append(block_diagonal(base))
        lasts.append(block_diagonal((base * weight).T))
    order = [p for u in range(quarter) for p in (u, half - u)] + [quarter]
    forward = []
    for p in order:
        cosine, sine = angle_tables(np.arange(LANES), p + blocks * np.arange(LANES), freq_len)
        forward.append(np.block([[cosine, -sine], [sine, cosine]]))
    forward = np.stack(forward).astype(ml_dtypes.bfloat16)
    return (np.stack(firsts), np.stack(lasts), forward)


def swap_lane_groups(pieces):
    count = len(pieces)
    width = LANES // count
    group = lax.broadcasted_iota(jnp.int32, pieces[0].shape, pieces[0].ndim - 1) // width
    results = []
    for g in range(count):
        total = None
        for k in range(count):
            shift = (width * (k - g)) % LANES
            moved = pieces[k] if shift == 0 else pltpu.roll(pieces[k], shift, pieces[k].ndim - 1)
            total = moved if total is None else jnp.where(group == k, moved, total)
        results.append(total)
    return results


def in_place(array):
    return pltpu.with_memory_space_constraint(array, pltpu.HBM)


def pack_kernel(
    gate_any, values_any, cotangent_any, taps_any, packed_ref, gate_ref, cotangent_ref,
    values_ref, taps_ref, arrived,
):
    pairs = (
        (values_any, values_ref),
        (cotangent_any, cotangent_ref),
        (gate_any, gate_ref),
        (taps_any, taps_ref),
    )
    chunks = arrived.shape[1]
    columns = taps_ref.shape[-1] // chunks
    per_peer = 32
    peers = columns // per_peer

    def copy(n, m):
        source, target = pairs[m]
        at = slice(n * columns, (n + 1) * columns)
        if m == 3:
            return pltpu.make_async_copy(source.at[:, at], target.at[:, at], arrived.at[m, n])
        return pltpu.make_async_copy(source.at[0, :, at], target.at[:, at], arrived.at[m, n])

    for n in range(chunks):
        for m in range(4):
            copy(n, m).start()
    for n in range(chunks):
        at = slice(n * columns, (n + 1) * columns)
        to = slice(n * peers, (n + 1) * peers)
        copy(n, 0).wait()
        packed_ref[to, 0:per_peer, :] = values_ref[:, at].T.reshape(peers, per_peer, LANES)
        copy(n, 1).wait()
        copy(n, 2).wait()
        grad = (cotangent_ref[:, at].astype(F32) * gate_ref[:, at].astype(F32)).astype(BF16)
        packed_ref[to, per_peer : 2 * per_peer, :] = grad.T.reshape(peers, per_peer, LANES)
        copy(n, 3).wait()
        taps = taps_ref[:, at]
        for block in range(columns // 512):
            start = 512 * block
            stacked = jnp.concatenate(
                [taps[:, start + LANES * i : start + LANES * (i + 1)] for i in range(4)], axis=0
            )
            turned = stacked.T.reshape(4, 4, 8, LANES)
            pieces = swap_lane_groups([turned[:, k] for k in range(4)])
            for i in range(4):
                first = n * peers + 16 * block + 4 * i
                packed_ref[first : first + 4, 2 * per_peer : 2 * per_peer + 8, :] = pieces[i].astype(BF16)


def pack(gate_input, values, cotangent, filter_taps):
    channels = values.shape[2]
    chunks = PACK_CHUNKS
    anywhere = pl.BlockSpec(memory_space=pltpu.HBM)
    return pl.pallas_call(
        pack_kernel,
        in_specs=[anywhere] * 4,
        out_specs=[pl.BlockSpec(memory_space=pltpu.VMEM)] * 3,
        out_shape=[
            jax.ShapeDtypeStruct((channels // 32, 72, LANES), BF16),
            jax.ShapeDtypeStruct((LANES, channels), BF16),
            jax.ShapeDtypeStruct((LANES, channels), BF16),
        ],
        scratch_shapes=[
            pltpu.VMEM((LANES, channels), BF16),
            pltpu.VMEM((32, channels), F32),
            pltpu.SemaphoreType.DMA((4, chunks)),
        ],
        compiler_params=pltpu.CompilerParams(vmem_limit_bytes=PACK_LIMIT),
        name="pack",
    )(*[in_place(x) for x in (gate_input, values, cotangent, filter_taps)])


def unpack_kernel(
    gate_ref, cotangent_ref, packed_ref, output_any, gate_grad_any, values_grad_any, taps_any,
    output_ref, gate_grad_ref, values_grad_ref, taps_ref, left,
):
    pairs = (
        (values_grad_ref, values_grad_any),
        (output_ref, output_any),
        (gate_grad_ref, gate_grad_any),
        (taps_ref, taps_any),
    )
    chunks = left.shape[1]
    columns = taps_ref.shape[-1] // chunks
    per_peer = 32
    peers = columns // per_peer

    def copy(n, m):
        source, target = pairs[m]
        at = slice(n * columns, (n + 1) * columns)
        if m == 3:
            return pltpu.make_async_copy(source.at[:, at], target.at[:, at], left.at[m, n])
        return pltpu.make_async_copy(source.at[:, at], target.at[0, :, at], left.at[m, n])

    for n in range(chunks):
        at = slice(n * columns, (n + 1) * columns)
        of = slice(n * peers, (n + 1) * peers)
        values_grad_ref[:, at] = packed_ref[of, per_peer : 2 * per_peer, :].reshape(columns, LANES).T
        copy(n, 0).start()
        conv = packed_ref[of, 0:per_peer, :].reshape(columns, LANES).T.astype(F32)
        output_ref[:, at] = (gate_ref[:, at].astype(F32) * conv).astype(BF16)
        copy(n, 1).start()
        gate_grad_ref[:, at] = (cotangent_ref[:, at].astype(F32) * conv).astype(BF16)
        copy(n, 2).start()
        taps = packed_ref[of, 2 * per_peer : 2 * per_peer + 8, :].astype(F32)
        for block in range(columns // 512):
            pieces = swap_lane_groups(
                [taps[16 * block + 4 * i : 16 * block + 4 * i + 4] for i in range(4)]
            )
            stacked = jnp.stack(pieces, axis=1).reshape(LANES, LANES).T
            for i in range(4):
                start = n * columns + 512 * block + LANES * i
                taps_ref[:, start : start + LANES] = stacked[32 * i : 32 * i + 32, :]
        copy(n, 3).start()
    for n in range(chunks):
        for m in range(4):
            copy(n, m).wait()


def unpack(gate_input, cotangent, packed):
    channels = gate_input.shape[1]
    chunks = UNPACK_CHUNKS
    within = pl.BlockSpec(memory_space=pltpu.VMEM)
    outside = pl.BlockSpec(memory_space=pltpu.HBM)
    wide_shape = jax.ShapeDtypeStruct((1, LANES, channels), BF16)
    return pl.pallas_call(
        unpack_kernel,
        in_specs=[within] * 3,
        out_specs=[outside] * 4,
        out_shape=[wide_shape, wide_shape, wide_shape, jax.ShapeDtypeStruct((32, channels), F32)],
        scratch_shapes=[
            pltpu.VMEM((LANES, channels), BF16),
            pltpu.VMEM((LANES, channels), BF16),
            pltpu.VMEM((LANES, channels), BF16),
            pltpu.VMEM((32, channels), F32),
            pltpu.SemaphoreType.DMA((4, chunks)),
        ],
        compiler_params=pltpu.CompilerParams(vmem_limit_bytes=PACK_LIMIT),
        name="unpack",
    )(gate_input, cotangent, packed)


def conv_kernel(
    data_ref, first_ref, last_ref, forward_ref, out_ref,
    filter_ref, signal_ref, mixed_ref,
):
    half = 32
    quarter = 16

    taps = data_ref[:, :, 64:72, :].astype(F32).reshape(8, 4, 4, 8, LANES)
    pieces = swap_lane_groups(
        [jnp.concatenate([taps[:, m, d] for d in range(4)], axis=0) for m in range(4)]
    )
    for k in range(4):
        filter_ref[:, 8 * k : 8 * k + 8, :] = pieces[k]

    def put(at, target, real, imag):
        signal_ref[at, target, 0:LANES] = real.astype(BF16)
        signal_ref[at, target, LANES : 2 * LANES] = imag.astype(BF16)

    def first_section(left, right, row):
        def parity_rows(parity):
            sides = [
                side.reshape(quarter, 2, PACK, LANES)[:, parity].reshape(quarter * PACK, LANES)
                for side in (left, right)
            ]
            return jnp.dot(
                first_ref[parity], jnp.concatenate(sides, axis=1), preferred_element_type=F32
            )

        even, odd = parity_rows(0), parity_rows(1)
        for side in range(2):
            lanes = slice(LANES * side, LANES * (side + 1))
            target = slice(row + PACK * side, row + PACK * side + PACK)
            even_0, odd_0 = even[0:PACK, lanes], odd[0:PACK, lanes]
            nothing = jnp.zeros((PACK, LANES), F32)
            put(0, target, even_0 + odd_0, nothing)
            put(1, target, even_0 - odd_0, nothing)
            put(half, target, even[PACK : 2 * PACK, lanes], odd[PACK : 2 * PACK, lanes])
            for u in range(1, quarter):
                at_r = slice(2 * u * PACK, (2 * u + 1) * PACK)
                at_i = slice((2 * u + 1) * PACK, (2 * u + 2) * PACK)
                even_r, even_i = even[at_r, lanes], even[at_i, lanes]
                odd_r, odd_i = odd[at_r, lanes], odd[at_i, lanes]
                put(2 * u, target, even_r + odd_r, even_i + odd_i)
                put(2 * u + 1, target, even_r - odd_r, odd_i - even_i)

    for t in range(8):
        column = (t // 4) * half
        left = data_ref[:, t % 4, column : column + PACK, :]
        right = data_ref[:, t % 4, column + PACK : column + 2 * PACK, :]
        first_section(left, right, t * half)
    first_section(
        filter_ref[:, 0:PACK, :].astype(BF16), filter_ref[:, PACK : 2 * PACK, :].astype(BF16), 256
    )

    def products(spec):
        filter_r, filter_i = spec[256:288, 0:LANES], spec[256:288, LANES:]
        conv_r, conv_i, back_r, back_i = [], [], [], []
        taps_r = taps_i = None
        for d in range(4):
            at = slice(32 * d, 32 * d + 32)
            value_r, value_i = spec[at, 0:LANES], spec[at, LANES:]
            at = slice(128 + 32 * d, 128 + 32 * d + 32)
            grad_r, grad_i = spec[at, 0:LANES], spec[at, LANES:]
            conv_r.append((value_r * filter_r - value_i * filter_i).astype(BF16))
            conv_i.append((value_r * filter_i + value_i * filter_r).astype(BF16))
            back_r.append((grad_r * filter_r + grad_i * filter_i).astype(BF16))
            back_i.append((grad_i * filter_r - grad_r * filter_i).astype(BF16))
            part_r = grad_r * value_r + grad_i * value_i
            part_i = grad_i * value_r - grad_r * value_i
            taps_r = part_r if d == 0 else taps_r + part_r
            taps_i = part_i if d == 0 else taps_i + part_i
        real = jnp.concatenate(conv_r + back_r + [taps_r.astype(BF16)], axis=0)
        imag = jnp.concatenate(conv_i + back_i + [taps_i.astype(BF16)], axis=0)
        return jnp.concatenate([real, imag], axis=1)

    def spectra(start, count):
        results = []
        for at in range(start, start + count):
            spec = jnp.dot(signal_ref[at], forward_ref[at], preferred_element_type=F32)
            mixture = lax.dot_general(
                products(spec),
                forward_ref[at],
                (((1,), (1,)), ((), ())),
                preferred_element_type=F32,
            )
            results.append((mixture[:, 0:LANES], mixture[:, LANES:]))
        return results

    ((middle_r, middle_i),) = spectra(half, 1)
    mixed_ref[0, 1] = middle_r.astype(BF16)
    mixed_ref[1, 1] = middle_i.astype(BF16)
    for u in range(quarter):
        (low_r, low_i), (high_r, high_i) = spectra(2 * u, 2)
        mixed_ref[0, 2 * u] = (low_r + high_r).astype(BF16)
        mixed_ref[1, 2 * u] = (low_r - high_r).astype(BF16)
        if u > 0:
            mixed_ref[0, 2 * u + 1] = (low_i - high_i).astype(BF16)
            mixed_ref[1, 2 * u + 1] = (low_i + high_i).astype(BF16)

    def last_section(row):
        results = []
        for parity in range(2):
            sides = [
                mixed_ref[parity, :, row + PACK * side : row + PACK * side + PACK, :].reshape(half * PACK, LANES)
                for side in range(2)
            ]
            part = jnp.dot(
                last_ref[parity], jnp.concatenate(sides, axis=1), preferred_element_type=F32
            )
            results.append(part.reshape(quarter, PACK, 2 * LANES))
        whole = jnp.stack(results, axis=1).reshape(half, PACK, 2 * LANES)
        return whole[:, :, 0:LANES], whole[:, :, LANES:]

    left, right = last_section(256)
    filter_ref[:, 0:PACK, :] = left
    filter_ref[:, PACK : 2 * PACK, :] = right
    pieces = swap_lane_groups([filter_ref[:, 8 * k : 8 * k + 8, :] for k in range(4)])
    for m in range(4):
        for d in range(4):
            part = pieces[m][8 * d : 8 * d + 8].astype(BF16)
            for high in range(8):
                out_ref[4 * high + m, d, 64:72, :] = part[high]
    for t in range(8):
        column = (t // 4) * half
        left, right = last_section(t * half)
        out_ref[:, t % 4, column : column + PACK, :] = left.astype(BF16)
        out_ref[:, t % 4, column + PACK : column + 2 * PACK, :] = right.astype(BF16)


def convolve(received, tables):
    whole = pl.BlockSpec(memory_space=pltpu.VMEM)
    return pl.pallas_call(
        conv_kernel,
        in_specs=[whole] * 4,
        out_specs=whole,
        out_shape=jax.ShapeDtypeStruct(received.shape, BF16),
        scratch_shapes=[
            pltpu.VMEM((32, 32, LANES), F32),
            pltpu.VMEM((33, 288, 2 * LANES), BF16),
            pltpu.VMEM((2, 32, 288, LANES), BF16),
        ],
        compiler_params=pltpu.CompilerParams(vmem_limit_bytes=CONV_LIMIT),
        name="convolve",
    )(received, *tables)


def exchange(blocks):
    return lax.all_to_all(blocks, ("ctx", "dp"), split_axis=0, concat_axis=0, tiled=True)


def on_device(tables, gate_input, values, cotangent, filter_taps):
    packed, gate_held, cotangent_held = pack(gate_input, values, cotangent, filter_taps)
    by_member = (lax.axis_size("ctx"), lax.axis_size("dp")) + packed.shape[1:]
    results = convolve(exchange(packed).reshape(by_member), tables)
    returned = exchange(results.reshape(packed.shape))
    return unpack(gate_held, cotangent_held, returned)


def solution(mesh):
    tables = dft_tables(64)
    specs = (
        P("dp", "ctx", None),
        P("dp", "ctx", None),
        P("dp", "ctx", None),
        P(("dp", "ctx"), None),
    )

    def program(gate_input, values, cotangent, filter_taps):
        body = functools.partial(on_device, tables)
        return jax.shard_map(
            lambda *args: tuple(body(*args)), mesh=mesh, in_specs=specs, out_specs=specs, check_vma=False
        )(*[in_place(x) for x in (gate_input, values, cotangent, filter_taps)])

    return program
```

```python
import functools
import math

import jax
import jax.numpy as jnp
import ml_dtypes
import numpy as np
from jax import lax
from jax.experimental import pallas as pl
from jax.experimental.pallas import tpu as pltpu
from jax.sharding import PartitionSpec as P

LANES = 128
PACK = 16
PACK_CHUNKS = 1
UNPACK_CHUNKS = 4
PACK_LIMIT = 16 * 1024 * 1024
CONV_LIMIT = 32 * 1024 * 1024
BF16 = jnp.bfloat16
F32 = jnp.float32


def angle_tables(top, bottom, period):
    angles = (np.outer(top, bottom) % period).astype(np.float64) * (2.0 * math.pi / period)
    return np.cos(angles).astype(np.float32), np.sin(angles).astype(np.float32)


def block_diagonal(table):
    eye = np.eye(PACK, dtype=np.float32)
    return np.kron(table, eye).astype(ml_dtypes.bfloat16)


def dft_tables(blocks):
    freq_len = blocks * LANES
    half = blocks // 2
    quarter = half // 2
    firsts, lasts = [], []
    for parity in range(2):
        places = np.arange(parity, half, 2)
        cosine, sine = angle_tables(np.arange(quarter + 1), places, blocks)
        base = np.zeros((half, quarter), np.float32)
        base[0] = cosine[0]
        base[1] = cosine[quarter] if parity == 0 else -sine[quarter]
        for p in range(1, quarter):
            base[2 * p] = cosine[p]
            base[2 * p + 1] = -sine[p]
        weight = np.full((half, 1), 2.0 / freq_len, np.float32)
        weight[0] = 1.0 / freq_len
        firsts.append(block_diagonal(base))
        lasts.append(block_diagonal((base * weight).T))
    order = [p for u in range(quarter) for p in (u, half - u)] + [quarter]
    forward = []
    for p in order:
        cosine, sine = angle_tables(np.arange(LANES), p + blocks * np.arange(LANES), freq_len)
        forward.append(np.block([[cosine, -sine], [sine, cosine]]))
    forward = np.stack(forward).astype(ml_dtypes.bfloat16)
    return (np.stack(firsts), np.stack(lasts), forward)


def swap_lane_groups(pieces):
    count = len(pieces)
    width = LANES // count
    group = lax.broadcasted_iota(jnp.int32, pieces[0].shape, pieces[0].ndim - 1) // width
    results = []
    for g in range(count):
        total = None
        for k in range(count):
            shift = (width * (k - g)) % LANES
            moved = pieces[k] if shift == 0 else pltpu.roll(pieces[k], shift, pieces[k].ndim - 1)
            total = moved if total is None else jnp.where(group == k, moved, total)
        results.append(total)
    return results


def in_place(array):
    return pltpu.with_memory_space_constraint(array, pltpu.HBM)


def pack_kernel(
    gate_any, values_any, cotangent_any, taps_any, packed_ref, gate_ref, cotangent_ref,
    values_ref, taps_ref, arrived,
):
    pairs = (
        (values_any, values_ref),
        (cotangent_any, cotangent_ref),
        (gate_any, gate_ref),
        (taps_any, taps_ref),
    )
    chunks = arrived.shape[1]
    columns = taps_ref.shape[-1] // chunks
    per_peer = 32
    peers = columns // per_peer

    def copy(n, m):
        source, target = pairs[m]
        at = slice(n * columns, (n + 1) * columns)
        if m == 3:
            return pltpu.make_async_copy(source.at[:, at], target.at[:, at], arrived.at[m, n])
        return pltpu.make_async_copy(source.at[0, :, at], target.at[:, at], arrived.at[m, n])

    for n in range(chunks):
        for m in range(4):
            copy(n, m).start()
    for n in range(chunks):
        at = slice(n * columns, (n + 1) * columns)
        to = slice(n * peers, (n + 1) * peers)
        copy(n, 0).wait()
        packed_ref[to, 0:per_peer, :] = values_ref[:, at].T.reshape(peers, per_peer, LANES)
        copy(n, 1).wait()
        copy(n, 2).wait()
        grad = (cotangent_ref[:, at].astype(F32) * gate_ref[:, at].astype(F32)).astype(BF16)
        packed_ref[to, per_peer : 2 * per_peer, :] = grad.T.reshape(peers, per_peer, LANES)
        copy(n, 3).wait()
        taps = taps_ref[:, at]
        for block in range(columns // 512):
            start = 512 * block
            stacked = jnp.concatenate(
                [taps[:, start + LANES * i : start + LANES * (i + 1)] for i in range(4)], axis=0
            )
            turned = stacked.T.reshape(4, 4, 8, LANES)
            pieces = swap_lane_groups([turned[:, k] for k in range(4)])
            for i in range(4):
                first = n * peers + 16 * block + 4 * i
                packed_ref[first : first + 4, 2 * per_peer : 2 * per_peer + 8, :] = pieces[i].astype(BF16)


def pack(gate_input, values, cotangent, filter_taps):
    channels = values.shape[2]
    chunks = PACK_CHUNKS
    anywhere = pl.BlockSpec(memory_space=pltpu.HBM)
    return pl.pallas_call(
        pack_kernel,
        in_specs=[anywhere] * 4,
        out_specs=[pl.BlockSpec(memory_space=pltpu.VMEM)] * 3,
        out_shape=[
            jax.ShapeDtypeStruct((channels // 32, 72, LANES), BF16),
            jax.ShapeDtypeStruct((LANES, channels), BF16),
            jax.ShapeDtypeStruct((LANES, channels), BF16),
        ],
        scratch_shapes=[
            pltpu.VMEM((LANES, channels), BF16),
            pltpu.VMEM((32, channels), F32),
            pltpu.SemaphoreType.DMA((4, chunks)),
        ],
        compiler_params=pltpu.CompilerParams(vmem_limit_bytes=PACK_LIMIT),
        name="pack",
    )(*[in_place(x) for x in (gate_input, values, cotangent, filter_taps)])


def unpack_kernel(
    gate_ref, cotangent_ref, packed_ref, output_any, gate_grad_any, values_grad_any, taps_any,
    output_ref, gate_grad_ref, values_grad_ref, taps_ref, left,
):
    pairs = (
        (values_grad_ref, values_grad_any),
        (output_ref, output_any),
        (gate_grad_ref, gate_grad_any),
        (taps_ref, taps_any),
    )
    chunks = left.shape[1]
    columns = taps_ref.shape[-1] // chunks
    per_peer = 32
    peers = columns // per_peer

    def copy(n, m):
        source, target = pairs[m]
        at = slice(n * columns, (n + 1) * columns)
        if m == 3:
            return pltpu.make_async_copy(source.at[:, at], target.at[:, at], left.at[m, n])
        return pltpu.make_async_copy(source.at[:, at], target.at[0, :, at], left.at[m, n])

    for n in range(chunks):
        at = slice(n * columns, (n + 1) * columns)
        of = slice(n * peers, (n + 1) * peers)
        values_grad_ref[:, at] = packed_ref[of, per_peer : 2 * per_peer, :].reshape(columns, LANES).T
        copy(n, 0).start()
        conv = packed_ref[of, 0:per_peer, :].reshape(columns, LANES).T.astype(F32)
        output_ref[:, at] = (gate_ref[:, at].astype(F32) * conv).astype(BF16)
        copy(n, 1).start()
        gate_grad_ref[:, at] = (cotangent_ref[:, at].astype(F32) * conv).astype(BF16)
        copy(n, 2).start()
        taps = packed_ref[of, 2 * per_peer : 2 * per_peer + 8, :].astype(F32)
        for block in range(columns // 512):
            pieces = swap_lane_groups(
                [taps[16 * block + 4 * i : 16 * block + 4 * i + 4] for i in range(4)]
            )
            stacked = jnp.stack(pieces, axis=1).reshape(LANES, LANES).T
            for i in range(4):
                start = n * columns + 512 * block + LANES * i
                taps_ref[:, start : start + LANES] = stacked[32 * i : 32 * i + 32, :]
        copy(n, 3).start()
    for n in range(chunks):
        for m in range(4):
            copy(n, m).wait()


def unpack(gate_input, cotangent, packed):
    channels = gate_input.shape[1]
    chunks = UNPACK_CHUNKS
    within = pl.BlockSpec(memory_space=pltpu.VMEM)
    outside = pl.BlockSpec(memory_space=pltpu.HBM)
    wide_shape = jax.ShapeDtypeStruct((1, LANES, channels), BF16)
    return pl.pallas_call(
        unpack_kernel,
        in_specs=[within] * 3,
        out_specs=[outside] * 4,
        out_shape=[wide_shape, wide_shape, wide_shape, jax.ShapeDtypeStruct((32, channels), F32)],
        scratch_shapes=[
            pltpu.VMEM((LANES, channels), BF16),
            pltpu.VMEM((LANES, channels), BF16),
            pltpu.VMEM((LANES, channels), BF16),
            pltpu.VMEM((32, channels), F32),
            pltpu.SemaphoreType.DMA((4, chunks)),
        ],
        compiler_params=pltpu.CompilerParams(vmem_limit_bytes=PACK_LIMIT),
        name="unpack",
    )(gate_input, cotangent, packed)


def conv_kernel(
    data_ref, first_ref, last_ref, forward_ref, out_ref,
    filter_ref, signal_ref, mixed_ref,
):
    half = 32
    quarter = 16

    taps = data_ref[:, :, 64:72, :].astype(F32).reshape(8, 4, 4, 8, LANES)
    pieces = swap_lane_groups(
        [jnp.concatenate([taps[:, m, d] for d in range(4)], axis=0) for m in range(4)]
    )
    for k in range(4):
        filter_ref[:, 8 * k : 8 * k + 8, :] = pieces[k]

    def put(at, target, real, imag):
        signal_ref[at, target, 0:LANES] = real.astype(BF16)
        signal_ref[at, target, LANES : 2 * LANES] = imag.astype(BF16)

    def first_section(left, right, row):
        def parity_rows(parity):
            sides = [
                side.reshape(quarter, 2, PACK, LANES)[:, parity].reshape(quarter * PACK, LANES)
                for side in (left, right)
            ]
            return jnp.dot(
                first_ref[parity], jnp.concatenate(sides, axis=1), preferred_element_type=F32
            )

        even, odd = parity_rows(0), parity_rows(1)
        for side in range(2):
            lanes = slice(LANES * side, LANES * (side + 1))
            target = slice(row + PACK * side, row + PACK * side + PACK)
            even_0, odd_0 = even[0:PACK, lanes], odd[0:PACK, lanes]
            nothing = jnp.zeros((PACK, LANES), F32)
            put(0, target, even_0 + odd_0, nothing)
            put(1, target, even_0 - odd_0, nothing)
            put(half, target, even[PACK : 2 * PACK, lanes], odd[PACK : 2 * PACK, lanes])
            for u in range(1, quarter):
                at_r = slice(2 * u * PACK, (2 * u + 1) * PACK)
                at_i = slice((2 * u + 1) * PACK, (2 * u + 2) * PACK)
                even_r, even_i = even[at_r, lanes], even[at_i, lanes]
                odd_r, odd_i = odd[at_r, lanes], odd[at_i, lanes]
                put(2 * u, target, even_r + odd_r, even_i + odd_i)
                put(2 * u + 1, target, even_r - odd_r, odd_i - even_i)

    for t in range(8):
        column = (t // 4) * half
        left = data_ref[:, t % 4, column : column + PACK, :]
        right = data_ref[:, t % 4, column + PACK : column + 2 * PACK, :]
        first_section(left, right, t * half)
    first_section(
        filter_ref[:, 0:PACK, :].astype(BF16), filter_ref[:, PACK : 2 * PACK, :].astype(BF16), 256
    )

    def products(spec):
        filter_r, filter_i = spec[256:288, 0:LANES], spec[256:288, LANES:]
        conv_r, conv_i, back_r, back_i = [], [], [], []
        taps_r = taps_i = None
        for d in range(4):
            at = slice(32 * d, 32 * d + 32)
            value_r, value_i = spec[at, 0:LANES], spec[at, LANES:]
            at = slice(128 + 32 * d, 128 + 32 * d + 32)
            grad_r, grad_i = spec[at, 0:LANES], spec[at, LANES:]
            conv_r.append((value_r * filter_r - value_i * filter_i).astype(BF16))
            conv_i.append((value_r * filter_i + value_i * filter_r).astype(BF16))
            back_r.append((grad_r * filter_r + grad_i * filter_i).astype(BF16))
            back_i.append((grad_i * filter_r - grad_r * filter_i).astype(BF16))
            part_r = grad_r * value_r + grad_i * value_i
            part_i = grad_i * value_r - grad_r * value_i
            taps_r = part_r if d == 0 else taps_r + part_r
            taps_i = part_i if d == 0 else taps_i + part_i
        real = jnp.concatenate(conv_r + back_r + [taps_r.astype(BF16)], axis=0)
        imag = jnp.concatenate(conv_i + back_i + [taps_i.astype(BF16)], axis=0)
        return jnp.concatenate([real, imag], axis=1)

    def spectra(start, count):
        results = []
        for at in range(start, start + count):
            spec = jnp.dot(signal_ref[at], forward_ref[at], preferred_element_type=F32)
            mixture = lax.dot_general(
                products(spec),
                forward_ref[at],
                (((1,), (1,)), ((), ())),
                preferred_element_type=F32,
            )
            results.append((mixture[:, 0:LANES], mixture[:, LANES:]))
        return results

    ((middle_r, middle_i),) = spectra(half, 1)
    mixed_ref[0, 1] = middle_r.astype(BF16)
    mixed_ref[1, 1] = middle_i.astype(BF16)
    for u in range(quarter):
        (low_r, low_i), (high_r, high_i) = spectra(2 * u, 2)
        mixed_ref[0, 2 * u] = (low_r + high_r).astype(BF16)
        mixed_ref[1, 2 * u] = (low_r - high_r).astype(BF16)
        if u > 0:
            mixed_ref[0, 2 * u + 1] = (low_i - high_i).astype(BF16)
            mixed_ref[1, 2 * u + 1] = (low_i + high_i).astype(BF16)

    def last_section(row):
        results = []
        for parity in range(2):
            sides = [
                mixed_ref[parity, :, row + PACK * side : row + PACK * side + PACK, :].reshape(half * PACK, LANES)
                for side in range(2)
            ]
            part = jnp.dot(
                last_ref[parity], jnp.concatenate(sides, axis=1), preferred_element_type=F32
            )
            results.append(part.reshape(quarter, PACK, 2 * LANES))
        whole = jnp.stack(results, axis=1).reshape(half, PACK, 2 * LANES)
        return whole[:, :, 0:LANES], whole[:, :, LANES:]

    left, right = last_section(256)
    filter_ref[:, 0:PACK, :] = left
    filter_ref[:, PACK : 2 * PACK, :] = right
    pieces = swap_lane_groups([filter_ref[:, 8 * k : 8 * k + 8, :] for k in range(4)])
    for m in range(4):
        for d in range(4):
            part = pieces[m][8 * d : 8 * d + 8].astype(BF16)
            for high in range(8):
                out_ref[4 * high + m, d, 64:72, :] = part[high]
    for t in range(8):
        column = (t // 4) * half
        left, right = last_section(t * half)
        out_ref[:, t % 4, column : column + PACK, :] = left.astype(BF16)
        out_ref[:, t % 4, column + PACK : column + 2 * PACK, :] = right.astype(BF16)


def convolve(received, tables):
    whole = pl.BlockSpec(memory_space=pltpu.VMEM)
    return pl.pallas_call(
        conv_kernel,
        in_specs=[whole] * 4,
        out_specs=whole,
        out_shape=jax.ShapeDtypeStruct(received.shape, BF16),
        scratch_shapes=[
            pltpu.VMEM((32, 32, LANES), F32),
            pltpu.VMEM((33, 288, 2 * LANES), BF16),
            pltpu.VMEM((2, 32, 288, LANES), BF16),
        ],
        compiler_params=pltpu.CompilerParams(vmem_limit_bytes=CONV_LIMIT),
        name="convolve",
    )(received, *tables)


def exchange(blocks):
    return lax.all_to_all(blocks, ("ctx", "dp"), split_axis=0, concat_axis=0, tiled=True)


def on_device(tables, gate_input, values, cotangent, filter_taps):
    packed, gate_held, cotangent_held = pack(gate_input, values, cotangent, filter_taps)
    by_member = (lax.axis_size("ctx"), lax.axis_size("dp")) + packed.shape[1:]
    results = convolve(exchange(packed).reshape(by_member), tables)
    returned = exchange(results.reshape(packed.shape))
    return unpack(gate_held, cotangent_held, returned)


def solution(mesh):
    tables = dft_tables(64)
    specs = (
        P("dp", "ctx", None),
        P("dp", "ctx", None),
        P("dp", "ctx", None),
        P(("dp", "ctx"), None),
    )

    def program(gate_input, values, cotangent, filter_taps):
        body = functools.partial(on_device, tables)
        return jax.shard_map(
            lambda *args: tuple(body(*args)), mesh=mesh, in_specs=specs, out_specs=specs, check_vma=False
        )(*[in_place(x) for x in (gate_input, values, cotangent, filter_taps)])

    return program
```

```python
import functools
import math

import jax
import jax.numpy as jnp
import ml_dtypes
import numpy as np
from jax import lax
from jax.experimental import pallas as pl
from jax.experimental.pallas import tpu as pltpu
from jax.sharding import PartitionSpec as P

LANES = 128
PACK = 16
PACK_CHUNKS = 1
UNPACK_CHUNKS = 4
PACK_LIMIT = 16 * 1024 * 1024
CONV_LIMIT = 32 * 1024 * 1024
BF16 = jnp.bfloat16
F32 = jnp.float32


def angle_tables(top, bottom, period):
    angles = (np.outer(top, bottom) % period).astype(np.float64) * (2.0 * math.pi / period)
    return np.cos(angles).astype(np.float32), np.sin(angles).astype(np.float32)


def block_diagonal(table):
    eye = np.eye(PACK, dtype=np.float32)
    return np.kron(table, eye).astype(ml_dtypes.bfloat16)


def frequency_order(half):
    quarter, eighth = half // 2, half // 4
    quads = [p for u in range(1, eighth) for p in (u, half - u, quarter - u, quarter + u)]
    return quads + [eighth, half - eighth, 0, half, quarter]


def dft_tables(blocks):
    freq_len = blocks * LANES
    half = blocks // 2
    quarter = half // 2
    firsts, lasts = [], []
    for parity in range(2):
        places = np.arange(parity, half, 2)
        cosine, sine = angle_tables(np.arange(quarter + 1), places, blocks)
        base = np.zeros((half, quarter), np.float32)
        base[0] = cosine[0]
        base[1] = cosine[quarter] if parity == 0 else -sine[quarter]
        for p in range(1, quarter):
            base[2 * p] = cosine[p]
            base[2 * p + 1] = -sine[p]
        firsts.append(block_diagonal(base))
    eighth = quarter // 2
    for residue in range(4):
        places = np.arange(residue, half, 4)
        cosine, sine = angle_tables(np.arange(eighth + 1), places, blocks)
        base = np.zeros((quarter, eighth), np.float32)
        base[0] = 0.5
        base[1] = sine[eighth] * -1.0 if residue == 2 else cosine[eighth]
        for p in range(1, eighth):
            base[2 * p] = cosine[p]
            base[2 * p + 1] = -sine[p]
        lasts.append(block_diagonal((base * (2.0 / freq_len)).T))
    order = frequency_order(half)
    forward = []
    for p in order:
        cosine, sine = angle_tables(np.arange(LANES), p + blocks * np.arange(LANES), freq_len)
        forward.append(np.block([[cosine, -sine], [sine, cosine]]))
    forward = np.stack(forward).astype(ml_dtypes.bfloat16)
    return (np.stack(firsts), np.stack(lasts), forward)


def swap_lane_groups(pieces):
    count = len(pieces)
    width = LANES // count
    group = lax.broadcasted_iota(jnp.int32, pieces[0].shape, pieces[0].ndim - 1) // width
    results = []
    for g in range(count):
        total = None
        for k in range(count):
            shift = (width * (k - g)) % LANES
            moved = pieces[k] if shift == 0 else pltpu.roll(pieces[k], shift, pieces[k].ndim - 1)
            total = moved if total is None else jnp.where(group == k, moved, total)
        results.append(total)
    return results


def in_place(array):
    return pltpu.with_memory_space_constraint(array, pltpu.HBM)


def pack_kernel(
    gate_any, values_any, cotangent_any, taps_any, packed_ref, gate_ref, cotangent_ref,
    values_ref, taps_ref, arrived,
):
    pairs = (
        (values_any, values_ref),
        (cotangent_any, cotangent_ref),
        (gate_any, gate_ref),
        (taps_any, taps_ref),
    )
    chunks = arrived.shape[1]
    columns = taps_ref.shape[-1] // chunks
    per_peer = 32
    peers = columns // per_peer

    def copy(n, m):
        source, target = pairs[m]
        at = slice(n * columns, (n + 1) * columns)
        if m == 3:
            return pltpu.make_async_copy(source.at[:, at], target.at[:, at], arrived.at[m, n])
        return pltpu.make_async_copy(source.at[0, :, at], target.at[:, at], arrived.at[m, n])

    for n in range(chunks):
        for m in range(4):
            copy(n, m).start()
    for n in range(chunks):
        at = slice(n * columns, (n + 1) * columns)
        to = slice(n * peers, (n + 1) * peers)
        copy(n, 0).wait()
        packed_ref[to, 0:per_peer, :] = values_ref[:, at].T.reshape(peers, per_peer, LANES)
        copy(n, 1).wait()
        copy(n, 2).wait()
        grad = (cotangent_ref[:, at].astype(F32) * gate_ref[:, at].astype(F32)).astype(BF16)
        packed_ref[to, per_peer : 2 * per_peer, :] = grad.T.reshape(peers, per_peer, LANES)
        copy(n, 3).wait()
        taps = taps_ref[:, at]
        for block in range(columns // 512):
            start = 512 * block
            stacked = jnp.concatenate(
                [taps[:, start + LANES * i : start + LANES * (i + 1)] for i in range(4)], axis=0
            )
            turned = stacked.T.reshape(4, 4, 8, LANES)
            pieces = swap_lane_groups([turned[:, k] for k in range(4)])
            for i in range(4):
                first = n * peers + 16 * block + 4 * i
                packed_ref[first : first + 4, 2 * per_peer : 2 * per_peer + 8, :] = pieces[i].astype(BF16)


def pack(gate_input, values, cotangent, filter_taps):
    channels = values.shape[2]
    chunks = PACK_CHUNKS
    anywhere = pl.BlockSpec(memory_space=pltpu.HBM)
    return pl.pallas_call(
        pack_kernel,
        in_specs=[anywhere] * 4,
        out_specs=[pl.BlockSpec(memory_space=pltpu.VMEM)] * 3,
        out_shape=[
            jax.ShapeDtypeStruct((channels // 32, 72, LANES), BF16),
            jax.ShapeDtypeStruct((LANES, channels), BF16),
            jax.ShapeDtypeStruct((LANES, channels), BF16),
        ],
        scratch_shapes=[
            pltpu.VMEM((LANES, channels), BF16),
            pltpu.VMEM((32, channels), F32),
            pltpu.SemaphoreType.DMA((4, chunks)),
        ],
        compiler_params=pltpu.CompilerParams(vmem_limit_bytes=PACK_LIMIT),
        name="pack",
    )(*[in_place(x) for x in (gate_input, values, cotangent, filter_taps)])


def unpack_kernel(
    gate_ref, cotangent_ref, packed_ref, output_any, gate_grad_any, values_grad_any, taps_any,
    output_ref, gate_grad_ref, values_grad_ref, taps_ref, left,
):
    pairs = (
        (values_grad_ref, values_grad_any),
        (output_ref, output_any),
        (gate_grad_ref, gate_grad_any),
        (taps_ref, taps_any),
    )
    chunks = left.shape[1]
    columns = taps_ref.shape[-1] // chunks
    per_peer = 32
    peers = columns // per_peer

    def copy(n, m):
        source, target = pairs[m]
        at = slice(n * columns, (n + 1) * columns)
        if m == 3:
            return pltpu.make_async_copy(source.at[:, at], target.at[:, at], left.at[m, n])
        return pltpu.make_async_copy(source.at[:, at], target.at[0, :, at], left.at[m, n])

    for n in range(chunks):
        at = slice(n * columns, (n + 1) * columns)
        of = slice(n * peers, (n + 1) * peers)
        values_grad_ref[:, at] = packed_ref[of, per_peer : 2 * per_peer, :].reshape(columns, LANES).T
        copy(n, 0).start()
        conv = packed_ref[of, 0:per_peer, :].reshape(columns, LANES).T.astype(F32)
        output_ref[:, at] = (gate_ref[:, at].astype(F32) * conv).astype(BF16)
        copy(n, 1).start()
        gate_grad_ref[:, at] = (cotangent_ref[:, at].astype(F32) * conv).astype(BF16)
        copy(n, 2).start()
        taps = packed_ref[of, 2 * per_peer : 2 * per_peer + 8, :].astype(F32)
        for block in range(columns // 512):
            pieces = swap_lane_groups(
                [taps[16 * block + 4 * i : 16 * block + 4 * i + 4] for i in range(4)]
            )
            stacked = jnp.stack(pieces, axis=1).reshape(LANES, LANES).T
            for i in range(4):
                start = n * columns + 512 * block + LANES * i
                taps_ref[:, start : start + LANES] = stacked[32 * i : 32 * i + 32, :]
        copy(n, 3).start()
    for n in range(chunks):
        for m in range(4):
            copy(n, m).wait()


def unpack(gate_input, cotangent, packed):
    channels = gate_input.shape[1]
    chunks = UNPACK_CHUNKS
    within = pl.BlockSpec(memory_space=pltpu.VMEM)
    outside = pl.BlockSpec(memory_space=pltpu.HBM)
    wide_shape = jax.ShapeDtypeStruct((1, LANES, channels), BF16)
    return pl.pallas_call(
        unpack_kernel,
        in_specs=[within] * 3,
        out_specs=[outside] * 4,
        out_shape=[wide_shape, wide_shape, wide_shape, jax.ShapeDtypeStruct((32, channels), F32)],
        scratch_shapes=[
            pltpu.VMEM((LANES, channels), BF16),
            pltpu.VMEM((LANES, channels), BF16),
            pltpu.VMEM((LANES, channels), BF16),
            pltpu.VMEM((32, channels), F32),
            pltpu.SemaphoreType.DMA((4, chunks)),
        ],
        compiler_params=pltpu.CompilerParams(vmem_limit_bytes=PACK_LIMIT),
        name="unpack",
    )(gate_input, cotangent, packed)


def conv_kernel(
    data_ref, first_ref, last_ref, forward_ref, out_ref,
    filter_ref, signal_ref, mixed_ref,
):
    half = 32
    quarter = 16

    taps = data_ref[:, :, 64:72, :].astype(F32).reshape(8, 4, 4, 8, LANES)
    pieces = swap_lane_groups(
        [jnp.concatenate([taps[:, m, d] for d in range(4)], axis=0) for m in range(4)]
    )
    for k in range(4):
        filter_ref[:, 8 * k : 8 * k + 8, :] = pieces[k]

    place = {p: at for at, p in enumerate(frequency_order(half))}

    def put(p, target, real, imag):
        at = place[p]
        signal_ref[at, target, 0:LANES] = real.astype(BF16)
        signal_ref[at, target, LANES : 2 * LANES] = imag.astype(BF16)

    def first_section(left, right, row):
        def parity_rows(parity):
            sides = [
                side.reshape(quarter, 2, PACK, LANES)[:, parity].reshape(quarter * PACK, LANES)
                for side in (left, right)
            ]
            return jnp.dot(
                first_ref[parity], jnp.concatenate(sides, axis=1), preferred_element_type=F32
            )

        even, odd = parity_rows(0), parity_rows(1)
        for side in range(2):
            lanes = slice(LANES * side, LANES * (side + 1))
            target = slice(row + PACK * side, row + PACK * side + PACK)
            even_0, odd_0 = even[0:PACK, lanes], odd[0:PACK, lanes]
            nothing = jnp.zeros((PACK, LANES), F32)
            put(0, target, even_0 + odd_0, nothing)
            put(half, target, even_0 - odd_0, nothing)
            put(quarter, target, even[PACK : 2 * PACK, lanes], odd[PACK : 2 * PACK, lanes])
            for u in range(1, quarter):
                at_r = slice(2 * u * PACK, (2 * u + 1) * PACK)
                at_i = slice((2 * u + 1) * PACK, (2 * u + 2) * PACK)
                even_r, even_i = even[at_r, lanes], even[at_i, lanes]
                odd_r, odd_i = odd[at_r, lanes], odd[at_i, lanes]
                put(u, target, even_r + odd_r, even_i + odd_i)
                put(half - u, target, even_r - odd_r, odd_i - even_i)

    for t in range(8):
        column = (t // 4) * half
        left = data_ref[:, t % 4, column : column + PACK, :]
        right = data_ref[:, t % 4, column + PACK : column + 2 * PACK, :]
        first_section(left, right, t * half)
    first_section(
        filter_ref[:, 0:PACK, :].astype(BF16), filter_ref[:, PACK : 2 * PACK, :].astype(BF16), 256
    )

    def products(spec):
        filter_r, filter_i = spec[256:288, 0:LANES], spec[256:288, LANES:]
        conv_r, conv_i, back_r, back_i = [], [], [], []
        taps_r = taps_i = None
        for d in range(4):
            at = slice(32 * d, 32 * d + 32)
            value_r, value_i = spec[at, 0:LANES], spec[at, LANES:]
            at = slice(128 + 32 * d, 128 + 32 * d + 32)
            grad_r, grad_i = spec[at, 0:LANES], spec[at, LANES:]
            conv_r.append((value_r * filter_r - value_i * filter_i).astype(BF16))
            conv_i.append((value_r * filter_i + value_i * filter_r).astype(BF16))
            back_r.append((grad_r * filter_r + grad_i * filter_i).astype(BF16))
            back_i.append((grad_i * filter_r - grad_r * filter_i).astype(BF16))
            part_r = grad_r * value_r + grad_i * value_i
            part_i = grad_i * value_r - grad_r * value_i
            taps_r = part_r if d == 0 else taps_r + part_r
            taps_i = part_i if d == 0 else taps_i + part_i
        real = jnp.concatenate(conv_r + back_r + [taps_r.astype(BF16)], axis=0)
        imag = jnp.concatenate(conv_i + back_i + [taps_i.astype(BF16)], axis=0)
        return jnp.concatenate([real, imag], axis=1)

    def spectrum(p):
        at = place[p]
        spec = jnp.dot(signal_ref[at], forward_ref[at], preferred_element_type=F32)
        mixture = lax.dot_general(
            products(spec),
            forward_ref[at],
            (((1,), (1,)), ((), ())),
            preferred_element_type=F32,
        )
        return mixture[:, 0:LANES], mixture[:, LANES:]

    def halves(p):
        (low_r, low_i), (high_r, high_i) = spectrum(p), spectrum(half - p)
        return low_r + high_r, low_i - high_i, low_r - high_r, low_i + high_i

    def mix(at, *parts):
        for residue in range(4):
            mixed_ref[residue, at] = parts[residue].astype(BF16)

    eighth = quarter // 2
    for u in range(1, eighth):
        even_r, even_i, odd_r, odd_i = halves(u)
        other_r, other_i, across_r, across_i = halves(quarter - u)
        mix(2 * u, even_r + other_r, odd_r - across_i, even_r - other_r, odd_r + across_i)
        mix(2 * u + 1, even_i - other_i, odd_i - across_r, even_i + other_i, odd_i + across_r)
    even_r, even_i, odd_r, odd_i = halves(eighth)
    mix(1, even_r, odd_r - odd_i, even_i, odd_r + odd_i)
    first, last = spectrum(0)[0], spectrum(half)[0]
    middle_r, middle_i = spectrum(quarter)
    even, odd = first + last, first - last
    mix(0, even + 2.0 * middle_r, odd - 2.0 * middle_i, even - 2.0 * middle_r, odd + 2.0 * middle_i)

    def last_section(row):
        results = []
        for residue in range(4):
            sides = [
                mixed_ref[residue, :, row + PACK * side : row + PACK * side + PACK, :].reshape(
                    quarter * PACK, LANES
                )
                for side in range(2)
            ]
            part = jnp.dot(
                last_ref[residue], jnp.concatenate(sides, axis=1), preferred_element_type=F32
            )
            results.append(part.reshape(eighth, PACK, 2 * LANES))
        whole = jnp.stack(results, axis=1).reshape(half, PACK, 2 * LANES)
        return whole[:, :, 0:LANES], whole[:, :, LANES:]

    left, right = last_section(256)
    filter_ref[:, 0:PACK, :] = left
    filter_ref[:, PACK : 2 * PACK, :] = right
    pieces = swap_lane_groups([filter_ref[:, 8 * k : 8 * k + 8, :] for k in range(4)])
    for m in range(4):
        for d in range(4):
            part = pieces[m][8 * d : 8 * d + 8].astype(BF16)
            for high in range(8):
                out_ref[4 * high + m, d, 64:72, :] = part[high]
    for t in range(8):
        column = (t // 4) * half
        left, right = last_section(t * half)
        out_ref[:, t % 4, column : column + PACK, :] = left.astype(BF16)
        out_ref[:, t % 4, column + PACK : column + 2 * PACK, :] = right.astype(BF16)


def convolve(received, tables):
    whole = pl.BlockSpec(memory_space=pltpu.VMEM)
    return pl.pallas_call(
        conv_kernel,
        in_specs=[whole] * 4,
        out_specs=whole,
        out_shape=jax.ShapeDtypeStruct(received.shape, BF16),
        scratch_shapes=[
            pltpu.VMEM((32, 32, LANES), F32),
            pltpu.VMEM((33, 288, 2 * LANES), BF16),
            pltpu.VMEM((4, 16, 288, LANES), BF16),
        ],
        compiler_params=pltpu.CompilerParams(vmem_limit_bytes=CONV_LIMIT),
        name="convolve",
    )(received, *tables)


def exchange(blocks):
    return lax.all_to_all(blocks, ("ctx", "dp"), split_axis=0, concat_axis=0, tiled=True)


def on_device(tables, gate_input, values, cotangent, filter_taps):
    packed, gate_held, cotangent_held = pack(gate_input, values, cotangent, filter_taps)
    by_member = (lax.axis_size("ctx"), lax.axis_size("dp")) + packed.shape[1:]
    results = convolve(exchange(packed).reshape(by_member), tables)
    returned = exchange(results.reshape(packed.shape))
    return unpack(gate_held, cotangent_held, returned)


def solution(mesh):
    tables = dft_tables(64)
    specs = (
        P("dp", "ctx", None),
        P("dp", "ctx", None),
        P("dp", "ctx", None),
        P(("dp", "ctx"), None),
    )

    def program(gate_input, values, cotangent, filter_taps):
        body = functools.partial(on_device, tables)
        return jax.shard_map(
            lambda *args: tuple(body(*args)), mesh=mesh, in_specs=specs, out_specs=specs, check_vma=False
        )(*[in_place(x) for x in (gate_input, values, cotangent, filter_taps)])

    return program
```

```python
import functools
import math

import jax
import jax.numpy as jnp
import ml_dtypes
import numpy as np
from jax import lax
from jax.experimental import pallas as pl
from jax.experimental.pallas import tpu as pltpu
from jax.sharding import PartitionSpec as P

LANES = 128
PACK = 16
PACK_CHUNKS = 1
UNPACK_CHUNKS = 4
PACK_LIMIT = 16 * 1024 * 1024
CONV_LIMIT = 32 * 1024 * 1024
BF16 = jnp.bfloat16
F32 = jnp.float32


def angle_tables(top, bottom, period):
    angles = (np.outer(top, bottom) % period).astype(np.float64) * (2.0 * math.pi / period)
    return np.cos(angles).astype(np.float32), np.sin(angles).astype(np.float32)


def block_diagonal(table):
    eye = np.eye(PACK, dtype=np.float32)
    return np.kron(table, eye).astype(ml_dtypes.bfloat16)


def frequency_order(half):
    quarter, eighth = half // 2, half // 4
    quads = [p for u in range(1, eighth) for p in (u, half - u, quarter - u, quarter + u)]
    return quads + [eighth, half - eighth, 0, half, quarter]


def dft_tables(blocks):
    freq_len = blocks * LANES
    half = blocks // 2
    quarter = half // 2
    firsts, lasts = [], []
    for parity in range(2):
        places = np.arange(parity, half, 2)
        cosine, sine = angle_tables(np.arange(quarter + 1), places, blocks)
        base = np.zeros((half, quarter), np.float32)
        base[0] = cosine[0]
        base[1] = cosine[quarter] if parity == 0 else -sine[quarter]
        for p in range(1, quarter):
            base[2 * p] = cosine[p]
            base[2 * p + 1] = -sine[p]
        firsts.append(block_diagonal(base))
    eighth = quarter // 2
    for residue in range(4):
        places = np.arange(residue, half, 4)
        cosine, sine = angle_tables(np.arange(eighth + 1), places, blocks)
        base = np.zeros((quarter, eighth), np.float32)
        base[0] = 0.5
        base[1] = sine[eighth] * -1.0 if residue == 2 else cosine[eighth]
        for p in range(1, eighth):
            base[2 * p] = cosine[p]
            base[2 * p + 1] = -sine[p]
        lasts.append(block_diagonal((base * (2.0 / freq_len)).T))
    order = frequency_order(half)
    forward = []
    for p in order:
        cosine, sine = angle_tables(np.arange(LANES), p + blocks * np.arange(LANES), freq_len)
        forward.append(np.block([[cosine, -sine], [sine, cosine]]))
    forward = np.stack(forward).astype(ml_dtypes.bfloat16)
    return (np.stack(firsts), np.stack(lasts), forward)


def swap_lane_groups(pieces):
    count = len(pieces)
    width = LANES // count
    group = lax.broadcasted_iota(jnp.int32, pieces[0].shape, pieces[0].ndim - 1) // width
    results = []
    for g in range(count):
        total = None
        for k in range(count):
            shift = (width * (k - g)) % LANES
            moved = pieces[k] if shift == 0 else pltpu.roll(pieces[k], shift, pieces[k].ndim - 1)
            total = moved if total is None else jnp.where(group == k, moved, total)
        results.append(total)
    return results


def in_place(array):
    return pltpu.with_memory_space_constraint(array, pltpu.HBM)


def pack_kernel(
    gate_any, values_any, cotangent_any, taps_any, packed_ref, gate_ref, cotangent_ref,
    values_ref, taps_ref, arrived,
):
    pairs = (
        (values_any, values_ref),
        (cotangent_any, cotangent_ref),
        (gate_any, gate_ref),
        (taps_any, taps_ref),
    )
    chunks = arrived.shape[1]
    columns = taps_ref.shape[-1] // chunks
    per_peer = 32
    peers = columns // per_peer

    def copy(n, m):
        source, target = pairs[m]
        at = slice(n * columns, (n + 1) * columns)
        if m == 3:
            return pltpu.make_async_copy(source.at[:, at], target.at[:, at], arrived.at[m, n])
        return pltpu.make_async_copy(source.at[0, :, at], target.at[:, at], arrived.at[m, n])

    for n in range(chunks):
        for m in range(4):
            copy(n, m).start()
    for n in range(chunks):
        at = slice(n * columns, (n + 1) * columns)
        to = slice(n * peers, (n + 1) * peers)
        copy(n, 0).wait()
        packed_ref[to, 0:per_peer, :] = values_ref[:, at].T.reshape(peers, per_peer, LANES)
        copy(n, 1).wait()
        copy(n, 2).wait()
        grad = (cotangent_ref[:, at].astype(F32) * gate_ref[:, at].astype(F32)).astype(BF16)
        packed_ref[to, per_peer : 2 * per_peer, :] = grad.T.reshape(peers, per_peer, LANES)
        copy(n, 3).wait()
        taps = taps_ref[:, at]
        for block in range(columns // 512):
            start = 512 * block
            stacked = jnp.concatenate(
                [taps[:, start + LANES * i : start + LANES * (i + 1)] for i in range(4)], axis=0
            )
            turned = stacked.T.reshape(4, 4, 8, LANES)
            pieces = swap_lane_groups([turned[:, k] for k in range(4)])
            for i in range(4):
                first = n * peers + 16 * block + 4 * i
                packed_ref[first : first + 4, 2 * per_peer : 2 * per_peer + 8, :] = pieces[i].astype(BF16)


def pack(gate_input, values, cotangent, filter_taps):
    channels = values.shape[2]
    chunks = PACK_CHUNKS
    anywhere = pl.BlockSpec(memory_space=pltpu.HBM)
    return pl.pallas_call(
        pack_kernel,
        in_specs=[anywhere] * 4,
        out_specs=[pl.BlockSpec(memory_space=pltpu.VMEM)] * 3,
        out_shape=[
            jax.ShapeDtypeStruct((channels // 32, 72, LANES), BF16),
            jax.ShapeDtypeStruct((LANES, channels), BF16),
            jax.ShapeDtypeStruct((LANES, channels), BF16),
        ],
        scratch_shapes=[
            pltpu.VMEM((LANES, channels), BF16),
            pltpu.VMEM((32, channels), F32),
            pltpu.SemaphoreType.DMA((4, chunks)),
        ],
        compiler_params=pltpu.CompilerParams(vmem_limit_bytes=PACK_LIMIT),
        name="pack",
    )(*[in_place(x) for x in (gate_input, values, cotangent, filter_taps)])


def unpack_kernel(
    gate_ref, cotangent_ref, packed_ref, output_any, gate_grad_any, values_grad_any, taps_any,
    output_ref, gate_grad_ref, values_grad_ref, taps_ref, left,
):
    pairs = (
        (values_grad_ref, values_grad_any),
        (output_ref, output_any),
        (gate_grad_ref, gate_grad_any),
        (taps_ref, taps_any),
    )
    chunks = left.shape[1]
    columns = taps_ref.shape[-1] // chunks
    per_peer = 32
    peers = columns // per_peer

    def copy(n, m):
        source, target = pairs[m]
        at = slice(n * columns, (n + 1) * columns)
        if m == 3:
            return pltpu.make_async_copy(source.at[:, at], target.at[:, at], left.at[m, n])
        return pltpu.make_async_copy(source.at[:, at], target.at[0, :, at], left.at[m, n])

    for n in range(chunks):
        at = slice(n * columns, (n + 1) * columns)
        of = slice(n * peers, (n + 1) * peers)
        values_grad_ref[:, at] = packed_ref[of, per_peer : 2 * per_peer, :].reshape(columns, LANES).T
        copy(n, 0).start()
        conv = packed_ref[of, 0:per_peer, :].reshape(columns, LANES).T.astype(F32)
        output_ref[:, at] = (gate_ref[:, at].astype(F32) * conv).astype(BF16)
        copy(n, 1).start()
        gate_grad_ref[:, at] = (cotangent_ref[:, at].astype(F32) * conv).astype(BF16)
        copy(n, 2).start()
        taps = packed_ref[of, 2 * per_peer : 2 * per_peer + 8, :].astype(F32)
        for block in range(columns // 512):
            pieces = swap_lane_groups(
                [taps[16 * block + 4 * i : 16 * block + 4 * i + 4] for i in range(4)]
            )
            stacked = jnp.stack(pieces, axis=1).reshape(LANES, LANES).T
            for i in range(4):
                start = n * columns + 512 * block + LANES * i
                taps_ref[:, start : start + LANES] = stacked[32 * i : 32 * i + 32, :]
        copy(n, 3).start()
    for n in range(chunks):
        for m in range(4):
            copy(n, m).wait()


def unpack(gate_input, cotangent, packed):
    channels = gate_input.shape[1]
    chunks = UNPACK_CHUNKS
    within = pl.BlockSpec(memory_space=pltpu.VMEM)
    outside = pl.BlockSpec(memory_space=pltpu.HBM)
    wide_shape = jax.ShapeDtypeStruct((1, LANES, channels), BF16)
    return pl.pallas_call(
        unpack_kernel,
        in_specs=[within] * 3,
        out_specs=[outside] * 4,
        out_shape=[wide_shape, wide_shape, wide_shape, jax.ShapeDtypeStruct((32, channels), F32)],
        scratch_shapes=[
            pltpu.VMEM((LANES, channels), BF16),
            pltpu.VMEM((LANES, channels), BF16),
            pltpu.VMEM((LANES, channels), BF16),
            pltpu.VMEM((32, channels), F32),
            pltpu.SemaphoreType.DMA((4, chunks)),
        ],
        compiler_params=pltpu.CompilerParams(vmem_limit_bytes=PACK_LIMIT),
        name="unpack",
    )(gate_input, cotangent, packed)


def conv_kernel(
    data_ref, first_ref, last_ref, forward_ref, out_ref,
    filter_ref, signal_ref, mixed_ref,
):
    half = 32
    quarter = 16

    taps = data_ref[:, :, 64:72, :].astype(F32).reshape(8, 4, 4, 8, LANES)
    pieces = swap_lane_groups(
        [jnp.concatenate([taps[:, m, d] for d in range(4)], axis=0) for m in range(4)]
    )
    for k in range(4):
        filter_ref[:, 8 * k : 8 * k + 8, :] = pieces[k]

    place = {p: at for at, p in enumerate(frequency_order(half))}

    def put(p, target, real, imag):
        at = place[p]
        signal_ref[at, target, 0:LANES] = real.astype(BF16)
        signal_ref[at, target, LANES : 2 * LANES] = imag.astype(BF16)

    def first_section(left, right, row):
        def parity_rows(parity):
            sides = [
                side.reshape(quarter, 2, PACK, LANES)[:, parity].reshape(quarter * PACK, LANES)
                for side in (left, right)
            ]
            return jnp.dot(
                first_ref[parity], jnp.concatenate(sides, axis=1), preferred_element_type=F32
            )

        even, odd = parity_rows(0), parity_rows(1)
        for side in range(2):
            lanes = slice(LANES * side, LANES * (side + 1))
            target = slice(row + PACK * side, row + PACK * side + PACK)
            even_0, odd_0 = even[0:PACK, lanes], odd[0:PACK, lanes]
            nothing = jnp.zeros((PACK, LANES), F32)
            put(0, target, even_0 + odd_0, nothing)
            put(half, target, even_0 - odd_0, nothing)
            put(quarter, target, even[PACK : 2 * PACK, lanes], odd[PACK : 2 * PACK, lanes])
            for u in range(1, quarter):
                at_r = slice(2 * u * PACK, (2 * u + 1) * PACK)
                at_i = slice((2 * u + 1) * PACK, (2 * u + 2) * PACK)
                even_r, even_i = even[at_r, lanes], even[at_i, lanes]
                odd_r, odd_i = odd[at_r, lanes], odd[at_i, lanes]
                put(u, target, even_r + odd_r, even_i + odd_i)
                put(half - u, target, even_r - odd_r, odd_i - even_i)

    for t in range(8):
        column = (t // 4) * half
        left = data_ref[:, t % 4, column : column + PACK, :]
        right = data_ref[:, t % 4, column + PACK : column + 2 * PACK, :]
        first_section(left, right, t * half)
    first_section(
        filter_ref[:, 0:PACK, :].astype(BF16), filter_ref[:, PACK : 2 * PACK, :].astype(BF16), 256
    )

    def products(spec):
        filter_r, filter_i = spec[256:288, 0:LANES], spec[256:288, LANES:]
        conv_r, conv_i, back_r, back_i = [], [], [], []
        taps_r = taps_i = None
        for d in range(4):
            at = slice(32 * d, 32 * d + 32)
            value_r, value_i = spec[at, 0:LANES], spec[at, LANES:]
            at = slice(128 + 32 * d, 128 + 32 * d + 32)
            grad_r, grad_i = spec[at, 0:LANES], spec[at, LANES:]
            conv_r.append((value_r * filter_r - value_i * filter_i).astype(BF16))
            conv_i.append((value_r * filter_i + value_i * filter_r).astype(BF16))
            back_r.append((grad_r * filter_r + grad_i * filter_i).astype(BF16))
            back_i.append((grad_i * filter_r - grad_r * filter_i).astype(BF16))
            part_r = grad_r * value_r + grad_i * value_i
            part_i = grad_i * value_r - grad_r * value_i
            taps_r = part_r if d == 0 else taps_r + part_r
            taps_i = part_i if d == 0 else taps_i + part_i
        real = jnp.concatenate(conv_r + back_r + [taps_r.astype(BF16)], axis=0)
        imag = jnp.concatenate(conv_i + back_i + [taps_i.astype(BF16)], axis=0)
        return jnp.concatenate([real, imag], axis=1)

    def spectrum(p):
        at = place[p]
        spec = jnp.dot(signal_ref[at], forward_ref[at], preferred_element_type=F32)
        mixture = lax.dot_general(
            products(spec),
            forward_ref[at],
            (((1,), (1,)), ((), ())),
            preferred_element_type=F32,
        )
        return mixture[:, 0:LANES], mixture[:, LANES:]

    def halves(p):
        (low_r, low_i), (high_r, high_i) = spectrum(p), spectrum(half - p)
        return low_r + high_r, low_i - high_i, low_r - high_r, low_i + high_i

    def mix(at, *parts):
        for residue in range(4):
            mixed_ref[residue, at] = parts[residue].astype(BF16)

    eighth = quarter // 2
    even_r, even_i, odd_r, odd_i = halves(eighth)
    mix(1, even_r, odd_r - odd_i, even_i, odd_r + odd_i)
    first, last = spectrum(0)[0], spectrum(half)[0]
    middle_r, middle_i = spectrum(quarter)
    even, odd = first + last, first - last
    mix(0, even + 2.0 * middle_r, odd - 2.0 * middle_i, even - 2.0 * middle_r, odd + 2.0 * middle_i)

    for u in range(1, eighth):
        even_r, even_i, odd_r, odd_i = halves(u)
        other_r, other_i, across_r, across_i = halves(quarter - u)
        mix(2 * u, even_r + other_r, odd_r - across_i, even_r - other_r, odd_r + across_i)
        mix(2 * u + 1, even_i - other_i, odd_i - across_r, even_i + other_i, odd_i + across_r)
    def last_section(row):
        results = []
        for residue in range(4):
            sides = [
                mixed_ref[residue, :, row + PACK * side : row + PACK * side + PACK, :].reshape(
                    quarter * PACK, LANES
                )
                for side in range(2)
            ]
            part = jnp.dot(
                last_ref[residue], jnp.concatenate(sides, axis=1), preferred_element_type=F32
            )
            results.append(part.reshape(eighth, PACK, 2 * LANES))
        whole = jnp.stack(results, axis=1).reshape(half, PACK, 2 * LANES)
        return whole[:, :, 0:LANES], whole[:, :, LANES:]

    left, right = last_section(256)
    filter_ref[:, 0:PACK, :] = left
    filter_ref[:, PACK : 2 * PACK, :] = right
    pieces = swap_lane_groups([filter_ref[:, 8 * k : 8 * k + 8, :] for k in range(4)])
    for m in range(4):
        for d in range(4):
            part = pieces[m][8 * d : 8 * d + 8].astype(BF16)
            for high in range(8):
                out_ref[4 * high + m, d, 64:72, :] = part[high]
    for t in range(8):
        column = (t // 4) * half
        left, right = last_section(t * half)
        out_ref[:, t % 4, column : column + PACK, :] = left.astype(BF16)
        out_ref[:, t % 4, column + PACK : column + 2 * PACK, :] = right.astype(BF16)


def convolve(received, tables):
    whole = pl.BlockSpec(memory_space=pltpu.VMEM)
    return pl.pallas_call(
        conv_kernel,
        in_specs=[whole] * 4,
        out_specs=whole,
        out_shape=jax.ShapeDtypeStruct(received.shape, BF16),
        scratch_shapes=[
            pltpu.VMEM((32, 32, LANES), F32),
            pltpu.VMEM((33, 288, 2 * LANES), BF16),
            pltpu.VMEM((4, 16, 288, LANES), BF16),
        ],
        compiler_params=pltpu.CompilerParams(vmem_limit_bytes=CONV_LIMIT),
        name="convolve",
    )(received, *tables)


def exchange(blocks):
    return lax.all_to_all(blocks, ("ctx", "dp"), split_axis=0, concat_axis=0, tiled=True)


def on_device(tables, gate_input, values, cotangent, filter_taps):
    packed, gate_held, cotangent_held = pack(gate_input, values, cotangent, filter_taps)
    by_member = (lax.axis_size("ctx"), lax.axis_size("dp")) + packed.shape[1:]
    results = convolve(exchange(packed).reshape(by_member), tables)
    returned = exchange(results.reshape(packed.shape))
    return unpack(gate_held, cotangent_held, returned)


def solution(mesh):
    tables = dft_tables(64)
    specs = (
        P("dp", "ctx", None),
        P("dp", "ctx", None),
        P("dp", "ctx", None),
        P(("dp", "ctx"), None),
    )

    def program(gate_input, values, cotangent, filter_taps):
        body = functools.partial(on_device, tables)
        return jax.shard_map(
            lambda *args: tuple(body(*args)), mesh=mesh, in_specs=specs, out_specs=specs, check_vma=False
        )(*[in_place(x) for x in (gate_input, values, cotangent, filter_taps)])

    return program
```
